32 devices in a mesh: node: 4 (over y, x), leaf: 8 (over z, core).
Axes of the slice: x: 2, y: 2, z: 4, core: 2. Of those that a mesh axis runs over, the one named last changes fastest.
Arguments:
- density: bfloat16 [128, 8, 128, 256], P('leaf', 'node'), parts along dimension 1, may hold values from -6 to 6
- near_tiles: bfloat16 [128, 6, 8, 128, 128], P('leaf', None, 'node'), parts along dimension 2, may hold values from -0.15625 to 0.15625
- neighbours: int32 [128, 6], P('leaf'), may hold values from 0 to 127, as said below
- counts: int32 [128], P('leaf'), may hold values from 3 to 6, as said below
- leaf_basis: bfloat16 [128, 8, 32, 128], P('leaf', 'node'), parts along dimension 1, may hold values from -0.375 to 0.375
- leaf_transfer: float32 [128, 8, 32, 32], P('leaf', 'node'), parts along dimension 1, may hold values from -0.1875 to 0.1875
- admissible: int32 [8, 7], P('leaf'), may hold values from 0 to 7, as said below
- top_out: float32 [8, 8, 32, 32], P('leaf', 'node'), parts along dimension 1, may hold values from -0.75 to 0.75
- top_in: float32 [8, 8, 32, 32], P('leaf', 'node'), parts along dimension 1, may hold values from -0.25 to 0.25
- coupling: float32 [8, 7, 8, 32, 32], P('leaf', None, 'node'), parts along dimension 2, may hold values from -0.25 to 0.25
- down_transfer: float32 [128, 8, 32, 32], P('leaf', 'node'), parts along dimension 1, may hold values from -0.75 to 0.75
- out_basis: bfloat16 [128, 8, 32, 128], P('leaf', 'node'), parts along dimension 1, may hold values from -0.75 to 0.75
Outputs:
- potential: bfloat16 [128, 8, 128, 256], P('leaf', 'node'), parts along dimension 1
The draws below stay inside these ranges and needn't reach their ends.
There are 4 independent parts, one for each index of `node`. The reference program is written for one: setup_inputs(seed, part) draws one part's arguments, and reference() takes and returns one part's arrays. A program takes and returns all parts, laid end to end along the dimension named above; an argument that names none is the same for every part. Nothing has to cross between parts.
Inputs may be any that keep to these rules, and one draw needn't show every extreme that they name: `neighbours`: slot 0 is the leaf itself; every neighbour lies within 4 leaf indices of its leaf; slots 1 and 2 are the leaves 4 below and above, clipped to the surface's range. `counts`: the number of live leading slots of each leaf. `admissible`: the 7 entries of row d are distinct and differ from d; slot 0 is d - 1 and slot 1 is d + 1, both modulo 8.
All inputs are finite; a program needn't handle non-finite values.
Results may differ from the reference program's by a relative error of at most 0.0045.
Values may be sent and summed in bfloat16 or wider, within the bound.
A program may use at most 128 MiB of HBM per device.

```python
import jax
import jax.numpy as jnp
from jax import lax

LEAVES_DEV = 16
B = 128
K = 32
RHS = 256
NEAR = 6
HALO = 4
SUBTREES = 8
LEAVES = 128
FAR = 7


def draw_neighbours(key, part):
    inner = jnp.concatenate([jnp.arange(-HALO + 1, 0, dtype=jnp.int32), jnp.arange(1, HALO, dtype=jnp.int32)])
    fixed_offsets = jnp.array([0, -HALO, HALO], dtype=jnp.int32)

    def one_leaf(leaf_key):
        order = jax.random.permutation(leaf_key, 2 * HALO - 2)[:NEAR - 3]
        return jnp.concatenate([fixed_offsets, inner[order]])
    offsets = jax.vmap(one_leaf)(jax.random.split(key, LEAVES))
    leaf_ids = jnp.arange(LEAVES, dtype=jnp.int32)[:, None]
    return jnp.clip(leaf_ids + offsets, 0, LEAVES - 1).astype(jnp.int32)


def draw_counts(key, part):
    load_key, extra_key, busy_key = jax.random.split(jax.random.fold_in(key, 7), 3)
    loads = jax.random.randint(load_key, (SUBTREES,), 0, NEAR - 2)
    extra = jax.random.randint(extra_key, (SUBTREES, LEAVES_DEV), 0, 1 << 20) % (loads[:, None] + 1)
    result = 3 + extra
    busiest = jax.random.randint(busy_key, (), 0, SUBTREES)
    subtree_ids = jnp.arange(SUBTREES)[:, None]
    leaf_ids = jnp.arange(LEAVES_DEV)[None, :]
    result = jnp.where((subtree_ids == busiest) & (leaf_ids == 0), NEAR, result)
    return result.reshape(LEAVES).astype(jnp.int32)


def draw_admissible(key, part):

    def one_subtree(sub_key, subtree):
        order = jax.random.permutation(sub_key, SUBTREES - 3)[:FAR - 2]
        rest = (subtree + 2 + order) % SUBTREES
        sides = jnp.stack([(subtree + SUBTREES - 1) % SUBTREES, (subtree + 1) % SUBTREES])
        return jnp.concatenate([sides, rest])
    keys = jax.random.split(jax.random.fold_in(key, 11), SUBTREES)
    return jax.vmap(one_subtree)(keys, jnp.arange(SUBTREES, dtype=jnp.int32)).astype(jnp.int32)


def levels(own_key, dims, cuts, low, high):
    gain, own = 1.0, jax.random.fold_in(own_key, 6)
    for dim, blocks in cuts:
        steps = jnp.exp(jax.random.uniform(jax.random.fold_in(own, dim), (blocks,), jnp.float32, low / len(cuts), high / len(cuts)))
        gain = gain * jnp.repeat(steps, dims[dim] // blocks).reshape([-1 if axis == dim else 1 for axis in range(len(dims))])
    return gain


def scatter_about(stream_key, shape, width, bound, cuts=(), held_as=jnp.bfloat16):
    drawn = jax.random.normal(stream_key, shape, jnp.float32) * width
    if len(cuts) > 0:
        drawn = levels(stream_key, shape, cuts, -0.22, 0.18) * drawn
    return jnp.clip(drawn, min=-bound, max=bound).astype(held_as)


def setup_inputs(seed: int = 0, part: int = 0) -> dict:
    streams_of = jax.random.split(jax.random.key(seed), 13)
    own_keys = jax.random.split(jax.random.fold_in(streams_of[12], part), 13)
    density = scatter_about(own_keys[0], (LEAVES, 2, B, RHS), 1.0, 6.0, ((0, 8),))
    near_tiles = scatter_about(own_keys[1], (LEAVES, NEAR, 2, B, B), (2 * B * NEAR) ** -0.5, 0.15625, ((0, 8),))
    neighbours = draw_neighbours(jax.random.fold_in(streams_of[12], 71), part)
    counts = draw_counts(jax.random.fold_in(streams_of[12], 71), part)
    leaf_basis = scatter_about(own_keys[4], (LEAVES, 2, K, B), (2 * B) ** -0.5, 0.375, ((0, 8),))
    leaf_transfer = scatter_about(own_keys[5], (LEAVES, 2, K, K), (2 * K * LEAVES_DEV) ** -0.5, 0.1875, ((0, 8),), jnp.float32)
    admissible = draw_admissible(jax.random.fold_in(streams_of[12], 71), part)
    top_out = scatter_about(own_keys[7], (SUBTREES, 2, K, K), (2 * K) ** -0.5, 0.75, ((0, 8),), jnp.float32)
    top_in = scatter_about(own_keys[8], (SUBTREES, 2, K, K), (2 * K * SUBTREES) ** -0.5, 0.25, ((0, 8),), jnp.float32)
    coupling = scatter_about(own_keys[9], (SUBTREES, FAR, 2, K, K), (2 * K * FAR) ** -0.5, 0.25, ((0, 8),), jnp.float32)
    down_transfer = scatter_about(own_keys[10], (LEAVES, 2, K, K), (2 * K) ** -0.5, 0.75, ((0, 8),), jnp.float32)
    out_basis = scatter_about(own_keys[11], (LEAVES, 2, K, B), (2 * K) ** -0.5, 0.75, ((0, 8),))
    return {"density": density, "near_tiles": near_tiles, "neighbours": neighbours, "counts": counts, "leaf_basis": leaf_basis, "leaf_transfer": leaf_transfer, "admissible": admissible, "top_out": top_out, "top_in": top_in, "coupling": coupling, "down_transfer": down_transfer, "out_basis": out_basis}


def complex_product(pattern, first, second, precision):
    def single(left_side, right_side):
        return jnp.einsum(pattern, left_side, right_side, precision=precision, preferred_element_type=jnp.float32)
    return (single(first[0], second[0]) - single(first[1], second[1]),
            single(first[0], second[1]) + single(first[1], second[0]))


def reference(density, near_tiles, neighbours, counts, leaf_basis, leaf_transfer, admissible, top_out, top_in, coupling, down_transfer, out_basis):
    highest = lax.Precision.HIGHEST
    dens_full = density.astype(jnp.float32)
    basis_full = leaf_basis.astype(jnp.float32)
    coef = complex_product('lkb,lbr->lkr', (basis_full[:, 0], basis_full[:, 1]), (dens_full[:, 0], dens_full[:, 1]), highest)
    coef = tuple(part.reshape(SUBTREES, LEAVES_DEV, K, RHS) for part in coef)
    upward = leaf_transfer.reshape(SUBTREES, LEAVES_DEV, 2, K, K)
    root = complex_product('dlij,dljr->dir', (upward[:, :, 0], upward[:, :, 1]), coef, highest)
    top_terms = complex_product('dij,djr->dir', (top_out[:, 0], top_out[:, 1]), root, highest)
    top = (jnp.sum(top_terms[0], axis=0), jnp.sum(top_terms[1], axis=0))
    picked = (root[0][admissible], root[1][admissible])
    far_field = complex_product('dfij,dfjr->dir', (coupling[:, :, 0], coupling[:, :, 1]), picked, highest)
    top_part = complex_product('dij,jr->dir', (top_in[:, 0], top_in[:, 1]), top, highest)
    far_field = (far_field[0] + top_part[0], far_field[1] + top_part[1])
    downward = down_transfer.reshape(SUBTREES, LEAVES_DEV, 2, K, K)
    down_pair = complex_product('dlij,djr->dlir', (downward[:, :, 0], downward[:, :, 1]), far_field, highest)
    down_coefs = jnp.stack([down_pair[0], down_pair[1]], axis=2).reshape(LEAVES, 2, K, RHS).astype(jnp.bfloat16)
    down_coefs = lax.optimization_barrier(down_coefs).astype(jnp.float32)
    out_full = out_basis.astype(jnp.float32)
    far_part = complex_product('lkb,lkr->lbr', (out_full[:, 0], out_full[:, 1]), (down_coefs[:, 0], down_coefs[:, 1]), highest)
    near_real = jnp.zeros((LEAVES, B, RHS), jnp.float32)
    near_imag = jnp.zeros((LEAVES, B, RHS), jnp.float32)
    for column in range(NEAR):
        pieces = density[neighbours[:, column]].astype(jnp.float32)
        tiles = near_tiles[:, column].astype(jnp.float32)
        term = complex_product('lab,lbr->lar', (tiles[:, 0], tiles[:, 1]), (pieces[:, 0], pieces[:, 1]), highest)
        live_mask = (counts > column).astype(jnp.float32)[:, None, None]
        near_real = near_real + live_mask * term[0]
        near_imag = near_imag + live_mask * term[1]
    return jnp.stack([far_part[0] + near_real, far_part[1] + near_imag], axis=1).astype(jnp.bfloat16)
```

```python
import functools

import jax
import jax.numpy as jnp
from jax import lax
from jax.experimental import pallas as pl
from jax.experimental.pallas import tpu as pltpu
from jax.sharding import PartitionSpec as P

HALO = 4
LIVE = 3
INDICES = (2, 3, 6)
MESH = pl.DeviceIdType.MESH
F32 = jnp.float32
BF16 = jnp.bfloat16


def mul(left, right):
    return jnp.dot(left, right, preferred_element_type=F32)


def split(x):
    high = x.astype(BF16)
    return high, (x - high.astype(F32)).astype(BF16)


def pack(real, imag):
    rh, rl = split(real)
    ih, il = split(imag)
    return jnp.concatenate([rh, ih, rl, il], axis=1)


def operand(real, imag):
    minus = -imag
    left = jnp.concatenate([real, minus, real, minus], axis=0)
    right = jnp.concatenate([imag, real, imag, real], axis=0)
    return jnp.concatenate([left, right], axis=1)


def embed(real, imag):
    return jnp.concatenate(
        [jnp.concatenate([real, -imag], axis=1), jnp.concatenate([imag, real], axis=1)], axis=0
    )


def kernel(
    n,
    density,
    near_tiles,
    neighbours_far,
    counts_far,
    leaf_basis_far,
    leaf_transfer_far,
    admissible_far,
    top_out_far,
    top_in_far,
    coupling_far,
    down_transfer_far,
    out_basis_far,
    near,
    coefs,
    turned,
    neighbours,
    counts,
    leaf_basis,
    leaf_transfer,
    admissible,
    top_out,
    top_in,
    coupling,
    down_transfer,
    out_basis,
    merged,
    downward,
    weights,
    partial,
    own,
    halo,
    sib,
    tiles,
    msg,
    small_sem,
    own_sem,
    tile_sem,
    cross_send,
    cross_recv,
    sib_send,
    sib_recv,
    up_send,
    up_recv,
    down_send,
    down_recv,
    pass_send,
    pass_recv,
    above_sem,
    far_sem,
):
    me = lax.axis_index("leaf")
    chips = n // 2
    chip = me // 2
    core = me % 2
    sibling = chip * 2 + (1 - core)
    leaves, _, panels, rhs = density.shape
    slots = near_tiles.shape[1]
    rank = leaf_basis.shape[2]
    far = coupling.shape[1]
    size = 2 * panels
    pair = 2 * rank
    chunks = leaves // HALO
    edge = leaves - HALO
    first = chip > 0
    last = chip < chips - 1

    own_copies = [
        pltpu.make_async_copy(
            density.at[pl.ds(k * HALO, HALO)], own.at[pl.ds(k * HALO, HALO)], own_sem.at[k]
        )
        for k in range(chunks)
    ]
    tile_copies = [
        pltpu.make_async_copy(
            near_tiles.at[pl.ds(k * HALO, HALO)], tiles.at[pl.ds(k * HALO, HALO)], tile_sem.at[k]
        )
        for k in range(chunks)
    ]

    small = [
        (leaf_basis_far, leaf_basis),
        (leaf_transfer_far, leaf_transfer),
        (top_out_far, top_out),
        (top_in_far, top_in),
        (coupling_far, coupling),
        (down_transfer_far, down_transfer),
        (out_basis_far, out_basis),
        (neighbours_far, neighbours),
        (counts_far, counts),
        (admissible_far, admissible),
    ]
    small_copies = [
        pltpu.make_async_copy(source, target, small_sem.at[k])
        for k, (source, target) in enumerate(small)
    ]

    def tell(semaphore, to):
        pl.semaphore_signal(semaphore, inc=1, device_id={"leaf": to}, device_id_type=MESH)

    def direct(step):
        return step % 2 == 1

    far_steps = [step for step in range(3, chips) if direct(step)]
    barrier = pltpu.get_barrier_semaphore()
    tell(barrier, sibling)

    @pl.when(last)
    def _():
        tell(barrier, (chip * 2 + 2) % n)
        tell(barrier, (chip * 2 + 3) % n)

    for step in far_steps:
        @pl.when(chip + step < chips)
        def _(step=step):
            tell(barrier, (me + 2 * step) % n)

    small_copies[0].start()
    small_copies[1].start()
    for copy in own_copies:
        copy.start()
    small_copies[2].start()
    small_copies[7].start()
    small_copies[8].start()
    for k in range(1, chunks - 1):
        tile_copies[k].start()

    def cross_copy(k):
        leaf = core * (leaves - 1 - k) + (1 - core) * k
        return pltpu.make_async_remote_copy(
            src_ref=density.at[pl.ds(leaf, 1)],
            dst_ref=halo.at[pl.ds(k, 1)],
            send_sem=cross_send.at[k],
            recv_sem=cross_recv.at[k],
            device_id={"leaf": (me + n - 1 + 2 * core) % n},
            device_id_type=MESH,
        )

    crossing = ((core == 0) & first) | ((core == 1) & last)

    sib_copy = pltpu.make_async_remote_copy(
        src_ref=density.at[pl.ds((1 - core) * edge, HALO)],
        dst_ref=sib,
        send_sem=sib_send.at[0],
        recv_sem=sib_recv.at[0],
        device_id={"leaf": sibling},
        device_id_type=MESH,
    )

    below = jnp.where(first, 2, 0)
    for step in far_steps:
        below += jnp.where(chip >= step, 1, 0)
    pl.semaphore_wait(barrier, 1 + below)

    @pl.when(first)
    def _():
        tell(above_sem, (chip * 2 + n - 2) % n)
        tell(above_sem, (chip * 2 + n - 1) % n)

    for step in far_steps:
        @pl.when(chip >= step)
        def _(step=step):
            tell(far_sem, (me + n - 2 * step) % n)

    @pl.when((core == 0) & first)
    def _():
        cross_copy(0).start()

    small_copies[0].wait()
    small_copies[1].wait()

    def merge(leaf, carry):
        basis = leaf_basis[leaf]
        t_high, t_low = split(leaf_transfer[leaf].reshape(pair, rank))
        value = mul(
            jnp.concatenate([t_high, t_low], axis=0),
            jnp.concatenate([basis[0], basis[1]], axis=1),
        )
        value = value[:pair] + value[pair:]
        real = value[:rank, :panels] - value[rank:, panels:]
        imag = value[:rank, panels:] + value[rank:, :panels]
        high, low = split(embed(real, imag))
        merged[leaf, :pair] = high
        merged[leaf, pair:] = low
        return carry

    lax.fori_loop(0, leaves, merge, 0, unroll=True)

    root = jnp.zeros((2 * pair, rhs), F32)
    for k in range(chunks):
        own_copies[k].wait()
        left = jnp.concatenate([merged[k * HALO + i] for i in range(HALO)], axis=1)
        root += mul(left, own[k * HALO : (k + 1) * HALO].reshape(HALO * size, rhs))
    small_copies[2].wait()
    packed = pack(top_out[0, 0], top_out[0, 1])
    msg[me, pair:] = jnp.concatenate([packed[: rank // 2], packed[rank // 2 :]], axis=1)
    msg[me, :pair] = (root[:pair] + root[pair:]).astype(BF16)

    def root_copy(slot, send, recv, to):
        return pltpu.make_async_remote_copy(
            src_ref=msg.at[slot],
            dst_ref=msg.at[slot],
            send_sem=send,
            recv_sem=recv,
            device_id={"leaf": to},
            device_id_type=MESH,
        )

    def chip_of(step):
        return (chip + n + step) % chips

    def line_copy(way, step, hop):
        send = (up_send, down_send)[way]
        recv = (up_recv, down_recv)[way]
        sign = (1, -1)[way]
        slot = chip_of(-sign * step) * 2 + core
        to = chip_of(sign * hop) * 2 + core
        return root_copy(slot, send.at[step + hop], recv.at[step + hop], to)

    def below_of(way, step):
        return (chip >= step) if way == 0 else (chip + step < chips)

    def pass_copy(step):
        return root_copy(
            chip_of(step) * 2 + core,
            pass_send.at[step % chips],
            pass_recv.at[step % chips],
            sibling,
        )

    for step in range(1, chips, 2):
        @pl.when(chip >= step)
        def _(step=step):
            line_copy(1, 0, step).start()

    @pl.when(last)
    def _():
        pl.semaphore_wait(above_sem, 2)
        line_copy(0, 0, 1).start()

    pass_copy(0).start()

    @pl.when((core == 1) & last)
    def _():
        cross_copy(0).start()
        cross_copy(1).start()

    @pl.when((core == 0) & first)
    def _():
        cross_copy(1).start()
        cross_copy(2).start()

    sib_copy.start()

    small_copies[6].start()
    for copy in small_copies[3:6] + small_copies[9:]:
        copy.start()
    tile_copies[0].start()
    tile_copies[chunks - 1].start()

    def arrive(way, step):
        @pl.when(below_of(way, step))
        def _():
            line_copy(way, 0, step).wait_recv()
            pass_copy((-step, step)[way]).start()

        if direct(step) and step < chips - 1:
            @pl.when(below_of(way, step) & below_of(1 - way, 1))
            def _():
                line_copy(way, step, 1).start()

    begin = me * leaves

    def inside(slot, leaf):
        return own[jnp.clip(neighbours[slot, leaf] - begin, 0, leaves - 1)]

    def beside(slot, leaf):
        place = neighbours[slot, leaf] - (begin + (1 - core) * leaves - core * HALO)
        piece = sib[jnp.clip(place, 0, HALO - 1)]
        if not isinstance(slot, int):
            return piece
        return jnp.where((place >= 0) & (place < HALO), piece, inside(slot, leaf))

    def across(k):
        def piece(slot, leaf):
            value = inside(slot, leaf)
            for j in range(k + 1) if isinstance(slot, int) else [k]:
                place = begin + core * (leaves + j) - (1 - core) * (1 + j)
                value = jnp.where(neighbours[slot, leaf] == place, halo[j], value)
            return value

        return piece

    def product(leaf, chosen):
        tops, bottoms, pieces = [], [], []
        for slot, piece in chosen:
            real = tiles[leaf, slot, 0]
            imag = tiles[leaf, slot, 1]
            if isinstance(slot, int) and slot >= LIVE:
                live = jnp.where(counts[leaf] > slot, 1.0, 0.0).astype(F32)
                live = jnp.full((panels, panels), live, F32).astype(BF16)
                real *= live
                imag *= live
            tops += [real, -imag]
            bottoms += [imag, real]
            pieces.append(piece(slot, leaf).reshape(size, rhs))
        left = jnp.concatenate(
            [jnp.concatenate(tops, axis=1), jnp.concatenate(bottoms, axis=1)], axis=0
        )
        return mul(left, jnp.concatenate(pieces, axis=0))

    def near_leaf(chosen, start=0):
        def body(step, carry):
            near[start + step] = product(start + step, chosen)
            return carry

        return body

    open_slots = list(range(LIVE, slots))
    every = [(slot, inside) for slot in range(slots)]
    small_copies[7].wait()
    small_copies[8].wait()
    middle = (chunks - 2) // 2
    for k in range(1, chunks - 1):
        tile_copies[k].wait()
        lax.fori_loop(k * HALO, (k + 1) * HALO, near_leaf(every), 0, unroll=2)
        if k == middle:
            arrive(0, 1)
            above = jnp.int32(0)
            for step in far_steps:
                above += jnp.where(chip + step < chips, 1, 0)
            if far_steps:
                @pl.when(chip + 3 < chips)
                def _():
                    pl.semaphore_wait(far_sem, above)

            for step in far_steps:
                @pl.when(chip + step < chips)
                def _(step=step):
                    line_copy(0, 0, step).start()

            @pl.when((core == 1) & last)
            def _():
                cross_copy(2).start()
                cross_copy(3).start()

    arrive(1, 1)

    @pl.when((core == 0) & first)
    def _():
        cross_copy(3).start()

    small_copies[6].wait()

    def turn(leaf, carry):
        basis = out_basis[leaf].astype(F32)
        left = jnp.concatenate([basis[0], -basis[1]], axis=0)
        right = jnp.concatenate([basis[1], basis[0]], axis=0)
        turned[leaf] = jnp.concatenate([left, right], axis=1).T.astype(BF16)
        return carry

    lax.fori_loop(0, leaves, turn, 0, unroll=2)

    for copy in small_copies[3:6] + small_copies[9:]:
        copy.wait()
    a_high, a_low = split(embed(top_in[0, 0], top_in[0, 1]))
    ones = lax.broadcasted_iota(jnp.int32, (pair, pair), 0) == lax.broadcasted_iota(
        jnp.int32, (pair, pair), 1
    )
    ones = jnp.where(ones, 1.0, 0.0).astype(BF16)
    spread = [
        jnp.concatenate([ones, a_high], axis=1),
        jnp.concatenate([jnp.zeros_like(ones), a_low], axis=1),
    ]
    some = HALO * pair

    def lower(k, carry):
        straight, turned_parts = [], []
        for i in range(HALO):
            real = down_transfer[k * HALO + i, 0].astype(BF16)
            imag = down_transfer[k * HALO + i, 1].astype(BF16)
            straight += [real, imag]
            turned_parts += [-imag, real]
        straight = jnp.concatenate(straight, axis=0)
        turned_parts = jnp.concatenate(turned_parts, axis=0)
        value = jnp.zeros((some, 2 * pair), F32)
        for right in spread:
            value += mul(straight, right[:rank]) + mul(turned_parts, right[rank:])
        rows = pl.ds(pl.multiple_of(k * some, some), some)
        downward[rows] = value.astype(BF16)
        return carry

    lax.fori_loop(0, chunks, lower, 0, unroll=2)

    for d in range(n):
        where = jnp.int32(0)
        found = jnp.int32(0)
        for slot in range(far):
            hit = admissible[0, slot] == d
            where = jnp.where(hit, slot, where)
            found = jnp.where(hit, 1, found)
        scale = found.astype(F32)
        weights[d] = pack(coupling[0, where, 0] * scale, coupling[0, where, 1] * scale)

    tile_copies[0].wait()
    tile_copies[chunks - 1].wait()
    sib_copy.wait_recv()
    chosen = [(0, inside), (1 + core, inside), (2 - core, beside)]
    chosen += [(slot, beside) for slot in open_slots]
    lax.fori_loop(0, HALO, near_leaf(chosen, (1 - core) * edge), 0, unroll=2)

    for step in range(2, chips):
        arrive(0, step)

    def terms(which):
        lefts, rights = [], []
        for k in range(2):
            value = msg[which * 2 + k]
            piece = value[pair:]
            top = jnp.concatenate([piece[:, : rhs // 2], piece[:, rhs // 2 :]], axis=0)
            lefts.append(jnp.concatenate([weights[which * 2 + k], top], axis=0))
            rights.append(operand(value[:rank], value[rank:pair]))
        return jnp.concatenate(lefts, axis=1), jnp.concatenate(rights, axis=0)

    def other(step):
        return jnp.where(last, step, chips - step) % chips

    pass_copy(0).wait_recv()
    pass_copy(other(1)).wait_recv()
    partial[...] = mul(*terms(chip)) + mul(*terms((chip + other(1)) % chips))

    chosen = [(0, inside), (2 - core, inside)]
    lax.fori_loop(0, HALO, near_leaf(chosen, core * edge), 0, unroll=2)

    for step in range(2, chips):
        arrive(1, step)
    for step in range(2, chips):
        pass_copy(other(step)).wait_recv()

    field = partial[...]
    for step in range(2, chips):
        field += mul(*terms((chip + other(step)) % chips))
    stacked = jnp.concatenate(
        [field[:rank, :rhs], field[:rank, rhs:], field[rank:, :rhs], field[rank:, rhs:]], axis=0
    )
    x = downward[...]
    coefs[...] = mul(
        jnp.concatenate([x, x], axis=1), jnp.concatenate(split(stacked), axis=0)
    ).astype(BF16)

    for k in range(HALO):
        @pl.when(crossing)
        def _(k=k):
            cross_copy(k).wait_recv()

        leaf = core * (edge + k) + (1 - core) * (HALO - 1 - k)
        chosen = [(slot, across(k)) for slot in [1 + core] + open_slots]
        near[leaf] += product(leaf, chosen)

    for k in range(HALO):
        @pl.when(crossing)
        def _(k=k):
            cross_copy(k).wait_send()
    sib_copy.wait_send()
    for way in range(2):
        for step in range(1, chips, 2):
            @pl.when(below_of(1 - way, step))
            def _(way=way, step=step):
                line_copy(way, 0, step).wait_send()
        for step in range(1, chips - 1, 2):
            @pl.when(below_of(way, step) & below_of(1 - way, 1))
            def _(way=way, step=step):
                line_copy(way, step, 1).wait_send()
    for step in range(chips):
        pass_copy(step).wait_send()


def finish(near, coefs, turned, out, staged, sem):
    leaves, _, panels, rhs = out.shape
    pair = turned.shape[2]
    copies = []
    for k in range(leaves // HALO):

        def body(leaf, carry):
            rows = pl.ds(pl.multiple_of(leaf * pair, pair), pair)
            value = mul(turned[leaf], coefs[rows]) + near[leaf]
            staged[leaf] = value.astype(BF16).reshape(2, panels, rhs)
            return carry

        lax.fori_loop(k * HALO, (k + 1) * HALO, body, 0, unroll=True)
        piece = pl.ds(k * HALO, HALO)
        copies.append(pltpu.make_async_copy(staged.at[piece], out.at[piece], sem.at[k]))
        copies[-1].start()
    for copy in copies:
        copy.wait()


def shards(*args):
    density, near_tiles = args[0], args[1]
    leaf_basis = args[4]
    n = lax.axis_size("leaf")
    leaves, _, panels, rhs = density.shape
    rank = leaf_basis.shape[2]
    pair = 2 * rank
    chips = n // 2
    chunks = leaves // HALO
    hbm = pl.BlockSpec(memory_space=pltpu.HBM)
    vmem = pl.BlockSpec(memory_space=pltpu.VMEM)
    dma = pltpu.SemaphoreType.DMA
    operands = [args[2].T if k == 2 else arg for k, arg in enumerate(args)]
    for k in range(len(operands)):
        operands[k] = pltpu.with_memory_space_constraint(operands[k], pltpu.HBM)
    middle = pl.pallas_call(
        functools.partial(kernel, n),
        out_shape=(
            jax.ShapeDtypeStruct((leaves, 2 * panels, rhs), F32),
            jax.ShapeDtypeStruct((leaves * pair, rhs), BF16),
            jax.ShapeDtypeStruct((leaves, 2 * panels, pair), BF16),
        ),
        in_specs=[hbm] * len(operands),
        out_specs=(vmem, vmem, vmem),
        scratch_shapes=[
            (pltpu.SMEM if k in INDICES else pltpu.VMEM)(operands[k].shape, operands[k].dtype)
            for k in range(2, len(operands))
        ]
        + [
            pltpu.VMEM((leaves, 2 * pair, 2 * panels), BF16),
            pltpu.VMEM((leaves * pair, 2 * pair), BF16),
            pltpu.VMEM((n, rank, 4 * rank), BF16),
            pltpu.VMEM((pair, 2 * rhs), F32),
            pltpu.VMEM(density.shape, BF16),
            pltpu.VMEM((HALO,) + density.shape[1:], BF16),
            pltpu.VMEM((HALO,) + density.shape[1:], BF16),
            pltpu.VMEM(near_tiles.shape, BF16),
            pltpu.VMEM((n, pair + rank // 2, rhs), BF16),
            dma((len(operands) - 2,)),
            dma((chunks,)),
            dma((chunks,)),
            dma((HALO,)),
            dma((HALO,)),
            dma((1,)),
            dma((1,)),
            dma((chips,)),
            dma((chips,)),
            dma((chips,)),
            dma((chips,)),
            dma((chips,)),
            dma((chips,)),
            pltpu.SemaphoreType.REGULAR,
            pltpu.SemaphoreType.REGULAR,
        ],
        compiler_params=pltpu.CompilerParams(
            collective_id=0, has_side_effects=True, vmem_limit_bytes=36 * 1024 * 1024
        ),
        name="exchange",
    )(*operands)
    return pl.pallas_call(
        finish,
        out_shape=jax.ShapeDtypeStruct(density.shape, BF16),
        in_specs=[vmem] * 3,
        out_specs=hbm,
        scratch_shapes=[pltpu.VMEM(density.shape, BF16), dma((chunks,))],
        compiler_params=pltpu.CompilerParams(vmem_limit_bytes=16 * 1024 * 1024),
        name="finish",
    )(*middle)


def solution(mesh):
    in_specs = (
        P("leaf", "node", None, None),
        P("leaf", None, "node", None, None),
        P("leaf", None),
        P("leaf"),
        P("leaf", "node", None, None),
        P("leaf", "node", None, None),
        P("leaf", None),
        P("leaf", "node", None, None),
        P("leaf", "node", None, None),
        P("leaf", None, "node", None, None),
        P("leaf", "node", None, None),
        P("leaf", "node", None, None),
    )
    out_specs = P("leaf", "node", None, None)
    return jax.shard_map(shards, mesh=mesh, in_specs=in_specs, out_specs=out_specs, check_vma=False)
```

```python
import functools

import jax
import jax.numpy as jnp
from jax import lax
from jax.experimental import pallas as pl
from jax.experimental.pallas import tpu as pltpu
from jax.sharding import PartitionSpec as P

HALO = 4
LIVE = 3
INDICES = (2, 3, 6)
MESH = pl.DeviceIdType.MESH
F32 = jnp.float32
BF16 = jnp.bfloat16


def mul(left, right):
    return jnp.dot(left, right, preferred_element_type=F32)


def split(x):
    high = x.astype(BF16)
    return high, (x - high.astype(F32)).astype(BF16)


def pack(real, imag):
    rh, rl = split(real)
    ih, il = split(imag)
    return jnp.concatenate([rh, ih, rl, il], axis=1)


def operand(real, imag):
    minus = -imag
    left = jnp.concatenate([real, minus, real, minus], axis=0)
    right = jnp.concatenate([imag, real, imag, real], axis=0)
    return jnp.concatenate([left, right], axis=1)


def embed(real, imag):
    return jnp.concatenate(
        [jnp.concatenate([real, -imag], axis=1), jnp.concatenate([imag, real], axis=1)], axis=0
    )


def kernel(
    n,
    density,
    near_tiles,
    neighbours_far,
    counts_far,
    leaf_basis_far,
    leaf_transfer_far,
    admissible_far,
    top_out_far,
    top_in_far,
    coupling_far,
    down_transfer_far,
    out_basis_far,
    near,
    coefs,
    turned,
    neighbours,
    counts,
    leaf_basis,
    leaf_transfer,
    admissible,
    top_out,
    top_in,
    coupling,
    down_transfer,
    out_basis,
    merged,
    downward,
    weights,
    partial,
    own,
    halo,
    sib,
    tiles,
    msg,
    small_sem,
    own_sem,
    tile_sem,
    cross_send,
    cross_recv,
    sib_send,
    sib_recv,
    up_send,
    up_recv,
    down_send,
    down_recv,
    pass_send,
    pass_recv,
    above_sem,
    far_sem,
):
    me = lax.axis_index("leaf")
    chips = n // 2
    chip = me // 2
    core = me % 2
    sibling = chip * 2 + (1 - core)
    leaves, _, panels, rhs = density.shape
    slots = near_tiles.shape[1]
    rank = leaf_basis.shape[2]
    far = coupling.shape[1]
    size = 2 * panels
    pair = 2 * rank
    chunks = leaves // HALO
    edge = leaves - HALO
    first = chip > 0
    last = chip < chips - 1

    own_copies = [
        pltpu.make_async_copy(
            density.at[pl.ds(k * HALO, HALO)], own.at[pl.ds(k * HALO, HALO)], own_sem.at[k]
        )
        for k in range(chunks)
    ]
    tile_copies = [
        pltpu.make_async_copy(
            near_tiles.at[pl.ds(k * HALO, HALO)], tiles.at[pl.ds(k * HALO, HALO)], tile_sem.at[k]
        )
        for k in range(chunks)
    ]

    small = [
        (leaf_basis_far, leaf_basis),
        (leaf_transfer_far, leaf_transfer),
        (top_out_far, top_out),
        (top_in_far, top_in),
        (coupling_far, coupling),
        (down_transfer_far, down_transfer),
        (out_basis_far, out_basis),
        (neighbours_far, neighbours),
        (counts_far, counts),
        (admissible_far, admissible),
    ]
    small_copies = [
        pltpu.make_async_copy(source, target, small_sem.at[k])
        for k, (source, target) in enumerate(small)
    ]

    def tell(semaphore, to):
        pl.semaphore_signal(semaphore, inc=1, device_id={"leaf": to}, device_id_type=MESH)

    def direct(step):
        return step % 2 == 1

    far_steps = [step for step in range(3, chips) if direct(step)]
    small_copies[0].start()
    small_copies[1].start()
    own_copies[0].start()
    own_copies[1].start()
    barrier = pltpu.get_barrier_semaphore()
    tell(barrier, sibling)

    @pl.when(last)
    def _():
        tell(barrier, (chip * 2 + 2) % n)
        tell(barrier, (chip * 2 + 3) % n)

    for step in range(2, chips):
        @pl.when((chip + step < chips) if direct(step) else (chip + step == chips - 1))
        def _(step=step):
            tell(barrier, (me + 2 * step) % n)


    def cross_copy(k, part):
        leaf = core * (leaves - 1 - k) + (1 - core) * k
        return pltpu.make_async_remote_copy(
            src_ref=density.at[pl.ds(leaf, 1), pl.ds(part, 1)],
            dst_ref=halo.at[pl.ds(k, 1), pl.ds(part, 1)],
            send_sem=cross_send.at[2 * k + part],
            recv_sem=cross_recv.at[2 * k + part],
            device_id={"leaf": (me + n - 1 + 2 * core) % n},
            device_id_type=MESH,
        )

    def cross_start(which, begin, end):
        @pl.when((core == which) & ((first, last)[which]))
        def _():
            for piece in range(begin, end):
                cross_copy(piece // 2, piece % 2).start()

    crossing = ((core == 0) & first) | ((core == 1) & last)

    sib_copy = pltpu.make_async_remote_copy(
        src_ref=density.at[pl.ds((1 - core) * edge, HALO)],
        dst_ref=sib,
        send_sem=sib_send.at[0],
        recv_sem=sib_recv.at[0],
        device_id={"leaf": sibling},
        device_id_type=MESH,
    )

    for copy in own_copies[2:] + [small_copies[2]]:
        copy.start()
    below = jnp.where(first, 2, 0)
    for step in range(2, chips):
        below += jnp.where(chip >= (step if direct(step) else chips - 1), 1, 0)
    pl.semaphore_wait(barrier, 1 + below)

    @pl.when(first)
    def _():
        tell(above_sem, (chip * 2 + n - 2) % n)
        tell(above_sem, (chip * 2 + n - 1) % n)

    for step in far_steps:
        @pl.when(chip >= step)
        def _(step=step):
            tell(far_sem, (me + n - 2 * step) % n)

    cross_start(0, 0, 3)
    small_copies[7].start()
    small_copies[8].start()
    for k in range(1, chunks - 1):
        tile_copies[k].start()
    small_copies[0].wait()
    small_copies[1].wait()

    def merge(leaf, carry):
        basis = leaf_basis[leaf]
        t_high, t_low = split(leaf_transfer[leaf].reshape(pair, rank))
        value = mul(
            jnp.concatenate([t_high, t_low], axis=0),
            jnp.concatenate([basis[0], basis[1]], axis=1),
        )
        value = value[:pair] + value[pair:]
        real = value[:rank, :panels] - value[rank:, panels:]
        imag = value[:rank, panels:] + value[rank:, :panels]
        high, low = split(embed(real, imag))
        merged[leaf, :pair] = high
        merged[leaf, pair:] = low
        return carry

    lax.fori_loop(0, leaves, merge, 0, unroll=True)

    root = jnp.zeros((2 * pair, rhs), F32)
    for k in range(chunks):
        if k == chunks - 1:
            @pl.when(last)
            def _():
                pl.semaphore_wait(above_sem, 2)

            cross_start(1, 0, 1)
        own_copies[k].wait()
        left = jnp.concatenate([merged[k * HALO + i] for i in range(HALO)], axis=1)
        root += mul(left, own[k * HALO : (k + 1) * HALO].reshape(HALO * size, rhs))
    small_copies[2].wait()
    packed = pack(top_out[0, 0], top_out[0, 1])
    msg[me, pair:] = jnp.concatenate([packed[: rank // 2], packed[rank // 2 :]], axis=1)
    msg[me, :pair] = (root[:pair] + root[pair:]).astype(BF16)

    def root_copy(slot, send, recv, to):
        return pltpu.make_async_remote_copy(
            src_ref=msg.at[slot],
            dst_ref=msg.at[slot],
            send_sem=send,
            recv_sem=recv,
            device_id={"leaf": to},
            device_id_type=MESH,
        )

    def chip_of(step):
        return (chip + n + step) % chips

    def line_copy(way, step, hop):
        send = (up_send, down_send)[way]
        recv = (up_recv, down_recv)[way]
        sign = (1, -1)[way]
        slot = chip_of(-sign * step) * 2 + core
        to = chip_of(sign * hop) * 2 + core
        return root_copy(slot, send.at[step + hop], recv.at[step + hop], to)

    def below_of(way, step):
        return (chip >= step) if way == 0 else (chip + step < chips)

    def pass_copy(step):
        return root_copy(
            chip_of(step) * 2 + core,
            pass_send.at[step % chips],
            pass_recv.at[step % chips],
            sibling,
        )

    def sends_down(step):
        return chip >= (step if direct(step) else chips - 1)

    for step in reversed(range(1, chips)):
        @pl.when(sends_down(step))
        def _(step=step):
            line_copy(1, 0, step).start()

    @pl.when(last)
    def _():
        line_copy(0, 0, 1).start()

    pass_copy(0).start()

    cross_start(1, 1, 4)
    cross_start(0, 3, 6)
    sib_copy.start()

    small_copies[6].start()
    for copy in small_copies[3:6] + small_copies[9:]:
        copy.start()
    tile_copies[0].start()
    tile_copies[chunks - 1].start()

    def relays(way, step):
        if way == 1:
            return (chip + step < chips - 1) & first
        return (chip >= step) & last

    def arrive(way, step):
        @pl.when(below_of(way, step))
        def _():
            line_copy(way, 0, step).wait_recv()
            pass_copy((-step, step)[way]).start()

        if direct(step) and step < chips - 1:
            @pl.when(relays(way, step))
            def _():
                line_copy(way, step, 1).start()

    begin = me * leaves

    def inside(slot, leaf):
        return own[jnp.clip(neighbours[slot, leaf] - begin, 0, leaves - 1)]

    def beside(slot, leaf):
        place = neighbours[slot, leaf] - (begin + (1 - core) * leaves - core * HALO)
        piece = sib[jnp.clip(place, 0, HALO - 1)]
        if not isinstance(slot, int):
            return piece
        return jnp.where((place >= 0) & (place < HALO), piece, inside(slot, leaf))

    def across(k):
        def piece(slot, leaf):
            value = inside(slot, leaf)
            for j in range(k + 1) if isinstance(slot, int) else [k]:
                place = begin + core * (leaves + j) - (1 - core) * (1 + j)
                value = jnp.where(neighbours[slot, leaf] == place, halo[j], value)
            return value

        return piece

    def product(leaf, chosen):
        tops, bottoms, pieces = [], [], []
        for slot, piece in chosen:
            real = tiles[leaf, slot, 0]
            imag = tiles[leaf, slot, 1]
            if isinstance(slot, int) and slot >= LIVE:
                live = jnp.where(counts[leaf] > slot, 1.0, 0.0).astype(F32)
                live = jnp.full((panels, panels), live, F32).astype(BF16)
                real *= live
                imag *= live
            tops += [real, -imag]
            bottoms += [imag, real]
            pieces.append(piece(slot, leaf).reshape(size, rhs))
        left = jnp.concatenate(
            [jnp.concatenate(tops, axis=1), jnp.concatenate(bottoms, axis=1)], axis=0
        )
        return mul(left, jnp.concatenate(pieces, axis=0))

    def near_leaf(chosen, start=0):
        def body(step, carry):
            near[start + step] = product(start + step, chosen)
            return carry

        return body

    open_slots = list(range(LIVE, slots))
    every = [(slot, inside) for slot in range(slots)]
    small_copies[7].wait()
    small_copies[8].wait()
    middle = (chunks - 2) // 2
    for k in range(1, chunks - 1):
        tile_copies[k].wait()
        lax.fori_loop(k * HALO, (k + 1) * HALO, near_leaf(every), 0, unroll=2)
        if k == middle:
            arrive(0, 1)
            above = jnp.int32(0)
            for step in far_steps:
                above += jnp.where(chip + step < chips, 1, 0)
            if far_steps:
                @pl.when(chip + 3 < chips)
                def _():
                    pl.semaphore_wait(far_sem, above)

            for step in far_steps:
                @pl.when(chip + step < chips)
                def _(step=step):
                    line_copy(0, 0, step).start()

            cross_start(1, 4, 2 * HALO)
            cross_start(0, 6, 7)

    tile_copies[0].wait()
    tile_copies[chunks - 1].wait()
    sib_copy.wait_recv()
    chosen = [(0, inside), (1 + core, inside), (2 - core, beside)]
    chosen += [(slot, beside) for slot in open_slots]
    lax.fori_loop(0, HALO, near_leaf(chosen, (1 - core) * edge), 0, unroll=2)
    arrive(1, 1)
    cross_start(0, 7, 2 * HALO)

    small_copies[6].wait()

    def turn(leaf, carry):
        basis = out_basis[leaf].astype(F32)
        left = jnp.concatenate([basis[0], -basis[1]], axis=0)
        right = jnp.concatenate([basis[1], basis[0]], axis=0)
        turned[leaf] = jnp.concatenate([left, right], axis=1).T.astype(BF16)
        return carry

    lax.fori_loop(0, leaves, turn, 0, unroll=2)

    for copy in small_copies[3:6] + small_copies[9:]:
        copy.wait()
    a_high, a_low = split(embed(top_in[0, 0], top_in[0, 1]))
    ones = lax.broadcasted_iota(jnp.int32, (pair, pair), 0) == lax.broadcasted_iota(
        jnp.int32, (pair, pair), 1
    )
    ones = jnp.where(ones, 1.0, 0.0).astype(BF16)
    spread = [
        jnp.concatenate([ones, a_high], axis=1),
        jnp.concatenate([jnp.zeros_like(ones), a_low], axis=1),
    ]
    some = HALO * pair

    def lower(k, carry):
        straight, turned_parts = [], []
        for i in range(HALO):
            real = down_transfer[k * HALO + i, 0].astype(BF16)
            imag = down_transfer[k * HALO + i, 1].astype(BF16)
            straight += [real, imag]
            turned_parts += [-imag, real]
        straight = jnp.concatenate(straight, axis=0)
        turned_parts = jnp.concatenate(turned_parts, axis=0)
        value = jnp.zeros((some, 2 * pair), F32)
        for right in spread:
            value += mul(straight, right[:rank]) + mul(turned_parts, right[rank:])
        rows = pl.ds(pl.multiple_of(k * some, some), some)
        downward[rows] = value.astype(BF16)
        return carry

    lax.fori_loop(0, chunks, lower, 0, unroll=2)

    for d in range(n):
        where = jnp.int32(0)
        found = jnp.int32(0)
        for slot in range(far):
            hit = admissible[0, slot] == d
            where = jnp.where(hit, slot, where)
            found = jnp.where(hit, 1, found)
        scale = found.astype(F32)
        weights[d] = pack(coupling[0, where, 0] * scale, coupling[0, where, 1] * scale)

    for step in range(2, chips):
        arrive(0, step)

    def terms(which):
        lefts, rights = [], []
        for k in range(2):
            value = msg[which * 2 + k]
            piece = value[pair:]
            top = jnp.concatenate([piece[:, : rhs // 2], piece[:, rhs // 2 :]], axis=0)
            lefts.append(jnp.concatenate([weights[which * 2 + k], top], axis=0))
            rights.append(operand(value[:rank], value[rank:pair]))
        return jnp.concatenate(lefts, axis=1), jnp.concatenate(rights, axis=0)

    def other(step):
        return jnp.where(last, step, chips - step) % chips

    pass_copy(0).wait_recv()
    pass_copy(other(1)).wait_recv()
    partial[...] = mul(*terms(chip)) + mul(*terms((chip + other(1)) % chips))

    chosen = [(0, inside), (2 - core, inside)]
    lax.fori_loop(0, HALO, near_leaf(chosen, core * edge), 0, unroll=2)

    def cross_leaf(k):
        @pl.when(crossing)
        def _():
            cross_copy(k, 0).wait_recv()
            cross_copy(k, 1).wait_recv()

        leaf = core * (edge + k) + (1 - core) * (HALO - 1 - k)
        chosen = [(slot, across(k)) for slot in [1 + core] + open_slots]
        near[leaf] += product(leaf, chosen)

    early = chip < chips // 2

    @pl.when(early)
    def _():
        for k in range(HALO - 2):
            cross_leaf(k)

    for step in range(2, chips):
        arrive(1, step)

    @pl.when(early)
    def _():
        cross_leaf(HALO - 2)

    for step in range(2, chips):
        pass_copy(other(step)).wait_recv()

    field = partial[...]
    for step in range(2, chips):
        field += mul(*terms((chip + other(step)) % chips))
    stacked = jnp.concatenate(
        [field[:rank, :rhs], field[:rank, rhs:], field[rank:, :rhs], field[rank:, rhs:]], axis=0
    )
    x = downward[...]
    coefs[...] = mul(
        jnp.concatenate([x, x], axis=1), jnp.concatenate(split(stacked), axis=0)
    ).astype(BF16)

    @pl.when(jnp.logical_not(early))
    def _():
        for k in range(HALO - 1):
            cross_leaf(k)

    cross_leaf(HALO - 1)

    for k in range(HALO):
        @pl.when(crossing)
        def _(k=k):
            cross_copy(k, 0).wait_send()
            cross_copy(k, 1).wait_send()
    sib_copy.wait_send()
    for step in range(1, chips):
        @pl.when(sends_down(step))
        def _(step=step):
            line_copy(1, 0, step).wait_send()

    for step in range(1, chips, 2):
        @pl.when(chip + step < chips)
        def _(step=step):
            line_copy(0, 0, step).wait_send()

    for way in range(2):
        for step in range(1, chips - 1, 2):
            @pl.when(relays(way, step))
            def _(way=way, step=step):
                line_copy(way, step, 1).wait_send()
    for step in range(chips):
        pass_copy(step).wait_send()


def finish(near, coefs, turned, out, staged, sem):
    leaves, _, panels, rhs = out.shape
    pair = turned.shape[2]
    copies = []
    for k in range(leaves // 2):

        def body(leaf, carry):
            rows = pl.ds(pl.multiple_of(leaf * pair, pair), pair)
            value = mul(turned[leaf], coefs[rows]) + near[leaf]
            staged[leaf] = value.astype(BF16).reshape(2, panels, rhs)
            return carry

        lax.fori_loop(k * 2, (k + 1) * 2, body, 0, unroll=True)
        piece = pl.ds(k * 2, 2)
        copies.append(pltpu.make_async_copy(staged.at[piece], out.at[piece], sem.at[k]))
        copies[-1].start()
    for copy in copies:
        copy.wait()


def shards(*args):
    density, near_tiles = args[0], args[1]
    leaf_basis = args[4]
    n = lax.axis_size("leaf")
    leaves, _, panels, rhs = density.shape
    rank = leaf_basis.shape[2]
    pair = 2 * rank
    chips = n // 2
    chunks = leaves // HALO
    hbm = pl.BlockSpec(memory_space=pltpu.HBM)
    vmem = pl.BlockSpec(memory_space=pltpu.VMEM)
    dma = pltpu.SemaphoreType.DMA
    operands = [args[2].T if k == 2 else arg for k, arg in enumerate(args)]
    for k in range(len(operands)):
        operands[k] = pltpu.with_memory_space_constraint(operands[k], pltpu.HBM)
    middle = pl.pallas_call(
        functools.partial(kernel, n),
        out_shape=(
            jax.ShapeDtypeStruct((leaves, 2 * panels, rhs), F32),
            jax.ShapeDtypeStruct((leaves * pair, rhs), BF16),
            jax.ShapeDtypeStruct((leaves, 2 * panels, pair), BF16),
        ),
        in_specs=[hbm] * len(operands),
        out_specs=(vmem, vmem, vmem),
        scratch_shapes=[
            (pltpu.SMEM if k in INDICES else pltpu.VMEM)(operands[k].shape, operands[k].dtype)
            for k in range(2, len(operands))
        ]
        + [
            pltpu.VMEM((leaves, 2 * pair, 2 * panels), BF16),
            pltpu.VMEM((leaves * pair, 2 * pair), BF16),
            pltpu.VMEM((n, rank, 4 * rank), BF16),
            pltpu.VMEM((pair, 2 * rhs), F32),
            pltpu.VMEM(density.shape, BF16),
            pltpu.VMEM((HALO,) + density.shape[1:], BF16),
            pltpu.VMEM((HALO,) + density.shape[1:], BF16),
            pltpu.VMEM(near_tiles.shape, BF16),
            pltpu.VMEM((n, pair + rank // 2, rhs), BF16),
            dma((len(operands) - 2,)),
            dma((chunks,)),
            dma((chunks,)),
            dma((2 * HALO,)),
            dma((2 * HALO,)),
            dma((1,)),
            dma((1,)),
            dma((chips,)),
            dma((chips,)),
            dma((chips,)),
            dma((chips,)),
            dma((chips,)),
            dma((chips,)),
            pltpu.SemaphoreType.REGULAR,
            pltpu.SemaphoreType.REGULAR,
        ],
        compiler_params=pltpu.CompilerParams(
            collective_id=0, has_side_effects=True, vmem_limit_bytes=36 * 1024 * 1024
        ),
        name="exchange",
    )(*operands)
    return pl.pallas_call(
        finish,
        out_shape=jax.ShapeDtypeStruct(density.shape, BF16),
        in_specs=[vmem] * 3,
        out_specs=hbm,
        scratch_shapes=[pltpu.VMEM(density.shape, BF16), dma((leaves // 2,))],
        compiler_params=pltpu.CompilerParams(vmem_limit_bytes=16 * 1024 * 1024),
        name="finish",
    )(*middle)


def solution(mesh):
    in_specs = (
        P("leaf", "node", None, None),
        P("leaf", None, "node", None, None),
        P("leaf", None),
        P("leaf"),
        P("leaf", "node", None, None),
        P("leaf", "node", None, None),
        P("leaf", None),
        P("leaf", "node", None, None),
        P("leaf", "node", None, None),
        P("leaf", None, "node", None, None),
        P("leaf", "node", None, None),
        P("leaf", "node", None, None),
    )
    out_specs = P("leaf", "node", None, None)
    return jax.shard_map(shards, mesh=mesh, in_specs=in_specs, out_specs=out_specs, check_vma=False)
```

```python
import functools

import jax
import jax.numpy as jnp
from jax import lax
from jax.experimental import pallas as pl
from jax.experimental.pallas import tpu as pltpu
from jax.sharding import PartitionSpec as P

HALO = 4
LIVE = 3
INDICES = (2, 3, 6)
MESH = pl.DeviceIdType.MESH
F32 = jnp.float32
BF16 = jnp.bfloat16


def mul(left, right):
    return jnp.dot(left, right, preferred_element_type=F32)


def split(x):
    high = x.astype(BF16)
    return high, (x - high.astype(F32)).astype(BF16)


def pack(real, imag):
    rh, rl = split(real)
    ih, il = split(imag)
    return jnp.concatenate([rh, ih, rl, il], axis=1)


def operand(real, imag):
    minus = -imag
    left = jnp.concatenate([real, minus, real, minus], axis=0)
    right = jnp.concatenate([imag, real, imag, real], axis=0)
    return jnp.concatenate([left, right], axis=1)


def embed(real, imag):
    return jnp.concatenate(
        [jnp.concatenate([real, -imag], axis=1), jnp.concatenate([imag, real], axis=1)], axis=0
    )


def kernel(
    n,
    density,
    near_tiles,
    neighbours_far,
    counts_far,
    leaf_basis_far,
    leaf_transfer_far,
    admissible_far,
    top_out_far,
    top_in_far,
    coupling_far,
    down_transfer_far,
    out_basis_far,
    near,
    coefs,
    turned,
    neighbours,
    counts,
    leaf_basis,
    leaf_transfer,
    admissible,
    top_out,
    top_in,
    coupling,
    down_transfer,
    out_basis,
    merged,
    downward,
    weights,
    partial,
    own,
    halo,
    sib,
    tiles,
    msg,
    small_sem,
    own_sem,
    tile_sem,
    cross_send,
    cross_recv,
    sib_send,
    sib_recv,
    up_send,
    up_recv,
    down_send,
    down_recv,
    pass_send,
    pass_recv,
    above_sem,
    far_sem,
):
    me = lax.axis_index("leaf")
    chips = n // 2
    chip = me // 2
    core = me % 2
    sibling = chip * 2 + (1 - core)
    leaves, _, panels, rhs = density.shape
    slots = near_tiles.shape[1]
    rank = leaf_basis.shape[2]
    far = coupling.shape[1]
    size = 2 * panels
    pair = 2 * rank
    chunks = leaves // HALO
    edge = leaves - HALO
    first = chip > 0
    last = chip < chips - 1

    own_copies = [
        pltpu.make_async_copy(
            density.at[pl.ds(k * HALO, HALO)], own.at[pl.ds(k * HALO, HALO)], own_sem.at[k]
        )
        for k in range(chunks)
    ]
    tile_copies = [
        pltpu.make_async_copy(
            near_tiles.at[pl.ds(k * HALO, HALO)], tiles.at[pl.ds(k * HALO, HALO)], tile_sem.at[k]
        )
        for k in range(chunks)
    ]

    small = [
        (leaf_basis_far, leaf_basis),
        (leaf_transfer_far, leaf_transfer),
        (top_out_far, top_out),
        (top_in_far, top_in),
        (coupling_far, coupling),
        (down_transfer_far, down_transfer),
        (out_basis_far, out_basis),
        (neighbours_far, neighbours),
        (counts_far, counts),
        (admissible_far, admissible),
    ]
    small_copies = [
        pltpu.make_async_copy(source, target, small_sem.at[k])
        for k, (source, target) in enumerate(small)
    ]

    def tell(semaphore, to):
        pl.semaphore_signal(semaphore, inc=1, device_id={"leaf": to}, device_id_type=MESH)

    def direct(step):
        return step % 2 == 1

    far_steps = [step for step in range(3, chips) if direct(step)]
    small_copies[0].start()
    small_copies[1].start()
    own_copies[0].start()
    own_copies[1].start()
    barrier = pltpu.get_barrier_semaphore()
    tell(barrier, sibling)

    @pl.when(last)
    def _():
        tell(barrier, (chip * 2 + 2) % n)
        tell(barrier, (chip * 2 + 3) % n)

    for step in range(2, chips):
        @pl.when((chip + step < chips) & (direct(step) | (core == 0) | (chip + step == chips - 1)))
        def _(step=step):
            tell(barrier, (me + 2 * step) % n)


    def cross_copy(k, part):
        leaf = core * (leaves - 1 - k) + (1 - core) * k
        return pltpu.make_async_remote_copy(
            src_ref=density.at[pl.ds(leaf, 1), pl.ds(part, 1)],
            dst_ref=halo.at[pl.ds(k, 1), pl.ds(part, 1)],
            send_sem=cross_send.at[2 * k + part],
            recv_sem=cross_recv.at[2 * k + part],
            device_id={"leaf": (me + n - 1 + 2 * core) % n},
            device_id_type=MESH,
        )

    def cross_start(which, begin, end):
        @pl.when((core == which) & ((first, last)[which]))
        def _():
            for piece in range(begin, end):
                cross_copy(piece // 2, piece % 2).start()

    crossing = ((core == 0) & first) | ((core == 1) & last)

    sib_copy = pltpu.make_async_remote_copy(
        src_ref=density.at[pl.ds((1 - core) * edge, HALO)],
        dst_ref=sib,
        send_sem=sib_send.at[0],
        recv_sem=sib_recv.at[0],
        device_id={"leaf": sibling},
        device_id_type=MESH,
    )

    for copy in own_copies[2:] + [small_copies[2]]:
        copy.start()
    def sends_down(step):
        return (chip >= step) & (direct(step) | (core == 0) | (chip == chips - 1))

    below = jnp.where(first, 2, 0)
    for step in range(2, chips):
        below += jnp.where(sends_down(step), 1, 0)
    pl.semaphore_wait(barrier, 1 + below)

    @pl.when(first)
    def _():
        tell(above_sem, (chip * 2 + n - 2) % n)
        tell(above_sem, (chip * 2 + n - 1) % n)

    for step in far_steps:
        @pl.when(chip >= step)
        def _(step=step):
            tell(far_sem, (me + n - 2 * step) % n)

    cross_start(0, 0, 3)
    small_copies[7].start()
    small_copies[8].start()
    for k in range(1, chunks - 1):
        tile_copies[k].start()
    small_copies[0].wait()
    small_copies[1].wait()

    def merge(leaf, carry):
        basis = leaf_basis[leaf]
        t_high, t_low = split(leaf_transfer[leaf].reshape(pair, rank))
        value = mul(
            jnp.concatenate([t_high, t_low], axis=0),
            jnp.concatenate([basis[0], basis[1]], axis=1),
        )
        value = value[:pair] + value[pair:]
        real = value[:rank, :panels] - value[rank:, panels:]
        imag = value[:rank, panels:] + value[rank:, :panels]
        high, low = split(embed(real, imag))
        merged[leaf, :pair] = high
        merged[leaf, pair:] = low
        return carry

    lax.fori_loop(0, leaves, merge, 0, unroll=True)

    root = jnp.zeros((2 * pair, rhs), F32)
    for k in range(chunks):
        if k == chunks - 1:
            @pl.when(last)
            def _():
                pl.semaphore_wait(above_sem, 2)

            cross_start(1, 0, 1)
        own_copies[k].wait()
        left = jnp.concatenate([merged[k * HALO + i] for i in range(HALO)], axis=1)
        root += mul(left, own[k * HALO : (k + 1) * HALO].reshape(HALO * size, rhs))
    small_copies[2].wait()
    packed = pack(top_out[0, 0], top_out[0, 1])
    msg[me, pair:] = jnp.concatenate([packed[: rank // 2], packed[rank // 2 :]], axis=1)
    msg[me, :pair] = (root[:pair] + root[pair:]).astype(BF16)

    def root_copy(slot, send, recv, to):
        return pltpu.make_async_remote_copy(
            src_ref=msg.at[slot],
            dst_ref=msg.at[slot],
            send_sem=send,
            recv_sem=recv,
            device_id={"leaf": to},
            device_id_type=MESH,
        )

    def chip_of(step):
        return (chip + n + step) % chips

    def line_copy(way, step, hop):
        send = (up_send, down_send)[way]
        recv = (up_recv, down_recv)[way]
        sign = (1, -1)[way]
        slot = chip_of(-sign * step) * 2 + core
        to = chip_of(sign * hop) * 2 + core
        return root_copy(slot, send.at[step + hop], recv.at[step + hop], to)

    def below_of(way, step):
        return (chip >= step) if way == 0 else (chip + step < chips)

    def pass_copy(step):
        return root_copy(
            chip_of(step) * 2 + core,
            pass_send.at[step % chips],
            pass_recv.at[step % chips],
            sibling,
        )

    for step in reversed(range(1, chips)):
        @pl.when(sends_down(step))
        def _(step=step):
            line_copy(1, 0, step).start()

    @pl.when(last)
    def _():
        line_copy(0, 0, 1).start()

    pass_copy(0).start()

    cross_start(1, 1, 4)
    cross_start(0, 3, 6)
    sib_copy.start()

    small_copies[6].start()
    for copy in small_copies[3:6] + small_copies[9:]:
        copy.start()
    tile_copies[0].start()
    tile_copies[chunks - 1].start()

    def relays(way, step):
        if way == 1:
            return (chip + step < chips - 1) & first & (core == 1)
        return (chip >= step) & last

    def arrive(way, step):
        @pl.when(below_of(way, step))
        def _():
            line_copy(way, 0, step).wait_recv()
            pass_copy((-step, step)[way]).start()

        if direct(step) and step < chips - 1:
            @pl.when(relays(way, step))
            def _():
                line_copy(way, step, 1).start()

    begin = me * leaves

    def inside(slot, leaf):
        return own[jnp.clip(neighbours[slot, leaf] - begin, 0, leaves - 1)]

    def beside(slot, leaf):
        place = neighbours[slot, leaf] - (begin + (1 - core) * leaves - core * HALO)
        piece = sib[jnp.clip(place, 0, HALO - 1)]
        if not isinstance(slot, int):
            return piece
        return jnp.where((place >= 0) & (place < HALO), piece, inside(slot, leaf))

    def across(k):
        def piece(slot, leaf):
            value = inside(slot, leaf)
            for j in range(k + 1) if isinstance(slot, int) else [k]:
                place = begin + core * (leaves + j) - (1 - core) * (1 + j)
                value = jnp.where(neighbours[slot, leaf] == place, halo[j], value)
            return value

        return piece

    def product(leaf, chosen):
        tops, bottoms, pieces = [], [], []
        for slot, piece in chosen:
            real = tiles[leaf, slot, 0]
            imag = tiles[leaf, slot, 1]
            if isinstance(slot, int) and slot >= LIVE:
                live = jnp.where(counts[leaf] > slot, 1.0, 0.0).astype(F32)
                live = jnp.full((panels, panels), live, F32).astype(BF16)
                real *= live
                imag *= live
            tops += [real, -imag]
            bottoms += [imag, real]
            pieces.append(piece(slot, leaf).reshape(size, rhs))
        left = jnp.concatenate(
            [jnp.concatenate(tops, axis=1), jnp.concatenate(bottoms, axis=1)], axis=0
        )
        return mul(left, jnp.concatenate(pieces, axis=0))

    def near_leaf(chosen, start=0):
        def body(step, carry):
            near[start + step] = product(start + step, chosen)
            return carry

        return body

    open_slots = list(range(LIVE, slots))
    every = [(slot, inside) for slot in range(slots)]
    small_copies[7].wait()
    small_copies[8].wait()
    for k in range(1, chunks - 1):
        tile_copies[k].wait()
        lax.fori_loop(k * HALO, (k + 1) * HALO, near_leaf(every), 0, unroll=True)

    arrive(0, 1)
    above = jnp.int32(0)
    for step in far_steps:
        above += jnp.where(chip + step < chips, 1, 0)
    if far_steps:
        @pl.when(chip + 3 < chips)
        def _():
            pl.semaphore_wait(far_sem, above)

    for step in far_steps:
        @pl.when(chip + step < chips)
        def _(step=step):
            line_copy(0, 0, step).start()

    cross_start(1, 4, 2 * HALO)
    cross_start(0, 6, 7)

    tile_copies[0].wait()
    tile_copies[chunks - 1].wait()
    sib_copy.wait_recv()
    chosen = [(0, inside), (1 + core, inside), (2 - core, beside)]
    chosen += [(slot, beside) for slot in open_slots]
    lax.fori_loop(0, HALO, near_leaf(chosen, (1 - core) * edge), 0, unroll=True)

    small_copies[6].wait()

    def turn(leaf, carry):
        basis = out_basis[leaf].astype(F32)
        left = jnp.concatenate([basis[0], -basis[1]], axis=0)
        right = jnp.concatenate([basis[1], basis[0]], axis=0)
        turned[leaf] = jnp.concatenate([left, right], axis=1).T.astype(BF16)
        return carry

    lax.fori_loop(0, leaves, turn, 0, unroll=8)
    arrive(1, 1)
    cross_start(0, 7, 2 * HALO)

    for copy in small_copies[3:6] + small_copies[9:]:
        copy.wait()
    a_high, a_low = split(embed(top_in[0, 0], top_in[0, 1]))
    ones = lax.broadcasted_iota(jnp.int32, (pair, pair), 0) == lax.broadcasted_iota(
        jnp.int32, (pair, pair), 1
    )
    ones = jnp.where(ones, 1.0, 0.0).astype(BF16)
    spread = [
        jnp.concatenate([ones, a_high], axis=1),
        jnp.concatenate([jnp.zeros_like(ones), a_low], axis=1),
    ]
    some = HALO * pair

    def lower(k, carry):
        straight, turned_parts = [], []
        for i in range(HALO):
            real = down_transfer[k * HALO + i, 0].astype(BF16)
            imag = down_transfer[k * HALO + i, 1].astype(BF16)
            straight += [real, imag]
            turned_parts += [-imag, real]
        straight = jnp.concatenate(straight, axis=0)
        turned_parts = jnp.concatenate(turned_parts, axis=0)
        value = jnp.zeros((some, 2 * pair), F32)
        for right in spread:
            value += mul(straight, right[:rank]) + mul(turned_parts, right[rank:])
        rows = pl.ds(pl.multiple_of(k * some, some), some)
        downward[rows] = value.astype(BF16)
        return carry

    lax.fori_loop(0, chunks, lower, 0, unroll=True)

    for d in range(n):
        where = jnp.int32(0)
        found = jnp.int32(0)
        for slot in range(far):
            hit = admissible[0, slot] == d
            where = jnp.where(hit, slot, where)
            found = jnp.where(hit, 1, found)
        scale = found.astype(F32)
        weights[d] = pack(coupling[0, where, 0] * scale, coupling[0, where, 1] * scale)

    for step in range(2, chips):
        arrive(0, step)

    def terms(which):
        lefts, rights = [], []
        for slot in which:
            value = msg[slot]
            piece = value[pair:]
            top = jnp.concatenate([piece[:, : rhs // 2], piece[:, rhs // 2 :]], axis=0)
            lefts.append(jnp.concatenate([weights[slot], top], axis=0))
            rights.append(operand(value[:rank], value[rank:pair]))
        return mul(jnp.concatenate(lefts, axis=1), jnp.concatenate(rights, axis=0))

    def other(step):
        return jnp.where(last, step, chips - step) % chips

    pass_copy(0).wait_recv()
    pass_copy(other(1)).wait_recv()
    beyond = (chip + other(1)) % chips
    partial[...] = terms([chip * 2, chip * 2 + 1, beyond * 2, beyond * 2 + 1])

    chosen = [(0, inside), (2 - core, inside)]
    lax.fori_loop(0, HALO, near_leaf(chosen, core * edge), 0, unroll=True)

    def cross_leaf(k):
        @pl.when(crossing)
        def _():
            cross_copy(k, 0).wait_recv()
            cross_copy(k, 1).wait_recv()

        leaf = core * (edge + k) + (1 - core) * (HALO - 1 - k)
        chosen = [(slot, across(k)) for slot in [1 + core] + open_slots]
        near[leaf] += product(leaf, chosen)

    early = (chip < chips // 2) | jnp.logical_not(crossing)

    @pl.when(early)
    def _():
        for k in range(HALO - 2):
            cross_leaf(k)

    for step in range(2, chips):
        arrive(1, step)

    @pl.when(early)
    def _():
        cross_leaf(HALO - 2)

    remote = [(chip + other(step)) % chips * 2 for step in range(2, chips)]
    if remote:
        partial[...] += terms([slot + core for slot in remote])
        for step in range(2, chips):
            pass_copy(other(step)).wait_recv()
    field = partial[...]
    if remote:
        field += terms([slot + 1 - core for slot in remote])
    stacked = jnp.concatenate(
        [field[:rank, :rhs], field[:rank, rhs:], field[rank:, :rhs], field[rank:, rhs:]], axis=0
    )
    x = downward[...]
    coefs[...] = mul(
        jnp.concatenate([x, x], axis=1), jnp.concatenate(split(stacked), axis=0)
    ).astype(BF16)

    @pl.when(jnp.logical_not(early))
    def _():
        for k in range(HALO - 1):
            cross_leaf(k)

    cross_leaf(HALO - 1)

    for k in range(HALO):
        @pl.when(crossing)
        def _(k=k):
            cross_copy(k, 0).wait_send()
            cross_copy(k, 1).wait_send()
    sib_copy.wait_send()
    for step in range(1, chips):
        @pl.when(sends_down(step))
        def _(step=step):
            line_copy(1, 0, step).wait_send()

    for step in range(1, chips, 2):
        @pl.when(chip + step < chips)
        def _(step=step):
            line_copy(0, 0, step).wait_send()

    for way in range(2):
        for step in range(1, chips - 1, 2):
            @pl.when(relays(way, step))
            def _(way=way, step=step):
                line_copy(way, step, 1).wait_send()
    for step in range(chips):
        pass_copy(step).wait_send()


def finish(near, coefs, turned, out, staged, sem):
    leaves, _, panels, rhs = out.shape
    pair = turned.shape[2]
    copies = []
    for k in range(leaves // 2):

        def body(leaf, carry):
            rows = pl.ds(pl.multiple_of(leaf * pair, pair), pair)
            value = mul(turned[leaf], coefs[rows]) + near[leaf]
            staged[leaf] = value.astype(BF16).reshape(2, panels, rhs)
            return carry

        lax.fori_loop(k * 2, (k + 1) * 2, body, 0, unroll=True)
        piece = pl.ds(k * 2, 2)
        copies.append(pltpu.make_async_copy(staged.at[piece], out.at[piece], sem.at[k]))
        copies[-1].start()
    for copy in copies:
        copy.wait()


def shards(*args):
    density, near_tiles = args[0], args[1]
    leaf_basis = args[4]
    n = lax.axis_size("leaf")
    leaves, _, panels, rhs = density.shape
    rank = leaf_basis.shape[2]
    pair = 2 * rank
    chips = n // 2
    chunks = leaves // HALO
    hbm = pl.BlockSpec(memory_space=pltpu.HBM)
    vmem = pl.BlockSpec(memory_space=pltpu.VMEM)
    dma = pltpu.SemaphoreType.DMA
    operands = [args[2].T if k == 2 else arg for k, arg in enumerate(args)]
    for k in range(len(operands)):
        operands[k] = pltpu.with_memory_space_constraint(operands[k], pltpu.HBM)
    middle = pl.pallas_call(
        functools.partial(kernel, n),
        out_shape=(
            jax.ShapeDtypeStruct((leaves, 2 * panels, rhs), F32),
            jax.ShapeDtypeStruct((leaves * pair, rhs), BF16),
            jax.ShapeDtypeStruct((leaves, 2 * panels, pair), BF16),
        ),
        in_specs=[hbm] * len(operands),
        out_specs=(vmem, vmem, vmem),
        scratch_shapes=[
            (pltpu.SMEM if k in INDICES else pltpu.VMEM)(operands[k].shape, operands[k].dtype)
            for k in range(2, len(operands))
        ]
        + [
            pltpu.VMEM((leaves, 2 * pair, 2 * panels), BF16),
            pltpu.VMEM((leaves * pair, 2 * pair), BF16),
            pltpu.VMEM((n, rank, 4 * rank), BF16),
            pltpu.VMEM((pair, 2 * rhs), F32),
            pltpu.VMEM(density.shape, BF16),
            pltpu.VMEM((HALO,) + density.shape[1:], BF16),
            pltpu.VMEM((HALO,) + density.shape[1:], BF16),
            pltpu.VMEM(near_tiles.shape, BF16),
            pltpu.VMEM((n, pair + rank // 2, rhs), BF16),
            dma((len(operands) - 2,)),
            dma((chunks,)),
            dma((chunks,)),
            dma((2 * HALO,)),
            dma((2 * HALO,)),
            dma((1,)),
            dma((1,)),
            dma((chips,)),
            dma((chips,)),
            dma((chips,)),
            dma((chips,)),
            dma((chips,)),
            dma((chips,)),
            pltpu.SemaphoreType.REGULAR,
            pltpu.SemaphoreType.REGULAR,
        ],
        compiler_params=pltpu.CompilerParams(
            collective_id=0, has_side_effects=True, vmem_limit_bytes=36 * 1024 * 1024
        ),
        name="exchange",
    )(*operands)
    return pl.pallas_call(
        finish,
        out_shape=jax.ShapeDtypeStruct(density.shape, BF16),
        in_specs=[vmem] * 3,
        out_specs=hbm,
        scratch_shapes=[pltpu.VMEM(density.shape, BF16), dma((leaves // 2,))],
        compiler_params=pltpu.CompilerParams(vmem_limit_bytes=16 * 1024 * 1024),
        name="finish",
    )(*middle)


def solution(mesh):
    in_specs = (
        P("leaf", "node", None, None),
        P("leaf", None, "node", None, None),
        P("leaf", None),
        P("leaf"),
        P("leaf", "node", None, None),
        P("leaf", "node", None, None),
        P("leaf", None),
        P("leaf", "node", None, None),
        P("leaf", "node", None, None),
        P("leaf", None, "node", None, None),
        P("leaf", "node", None, None),
        P("leaf", "node", None, None),
    )
    out_specs = P("leaf", "node", None, None)
    return jax.shard_map(shards, mesh=mesh, in_specs=in_specs, out_specs=out_specs, check_vma=False)
```

```python
import functools

import jax
import jax.numpy as jnp
from jax import lax
from jax.experimental import pallas as pl
from jax.experimental.pallas import tpu as pltpu
from jax.sharding import PartitionSpec as P

HALO = 4
LIVE = 3
INDICES = (2, 3, 6)
MESH = pl.DeviceIdType.MESH
F32 = jnp.float32
BF16 = jnp.bfloat16


def mul(left, right):
    return jnp.dot(left, right, preferred_element_type=F32)


def split(x):
    high = x.astype(BF16)
    return high, (x - high.astype(F32)).astype(BF16)


def pack(real, imag):
    rh, rl = split(real)
    ih, il = split(imag)
    return jnp.concatenate([rh, ih, rl, il], axis=1)


def operand(real, imag):
    minus = -imag
    left = jnp.concatenate([real, minus, real, minus], axis=0)
    right = jnp.concatenate([imag, real, imag, real], axis=0)
    return jnp.concatenate([left, right], axis=1)


def embed(real, imag):
    return jnp.concatenate(
        [jnp.concatenate([real, -imag], axis=1), jnp.concatenate([imag, real], axis=1)], axis=0
    )


def kernel(
    n,
    density,
    near_tiles,
    neighbours_far,
    counts_far,
    leaf_basis_far,
    leaf_transfer_far,
    admissible_far,
    top_out_far,
    top_in_far,
    coupling_far,
    down_transfer_far,
    out_basis_far,
    near,
    coefs,
    turned,
    neighbours,
    counts,
    leaf_basis,
    leaf_transfer,
    admissible,
    top_out,
    top_in,
    coupling,
    down_transfer,
    out_basis,
    merged,
    downward,
    weights,
    partial,
    own,
    halo,
    sib,
    tiles,
    msg,
    small_sem,
    own_sem,
    tile_sem,
    cross_send,
    cross_recv,
    sib_send,
    sib_recv,
    up_send,
    up_recv,
    down_send,
    down_recv,
    pass_send,
    pass_recv,
    above_sem,
    far_sem,
):
    me = lax.axis_index("leaf")
    chips = n // 2
    chip = me // 2
    core = me % 2
    sibling = chip * 2 + (1 - core)
    leaves, _, panels, rhs = density.shape
    slots = near_tiles.shape[1]
    rank = leaf_basis.shape[2]
    far = coupling.shape[1]
    size = 2 * panels
    pair = 2 * rank
    chunks = leaves // HALO
    edge = leaves - HALO
    first = chip > 0
    last = chip < chips - 1

    own_copies = [
        pltpu.make_async_copy(
            density.at[pl.ds(k * HALO, HALO)], own.at[pl.ds(k * HALO, HALO)], own_sem.at[k]
        )
        for k in range(chunks)
    ]
    tile_copies = [
        pltpu.make_async_copy(
            near_tiles.at[pl.ds(k * HALO, HALO)], tiles.at[pl.ds(k * HALO, HALO)], tile_sem.at[k]
        )
        for k in range(chunks)
    ]

    small = [
        (leaf_basis_far, leaf_basis),
        (leaf_transfer_far, leaf_transfer),
        (top_out_far, top_out),
        (top_in_far, top_in),
        (coupling_far, coupling),
        (down_transfer_far, down_transfer),
        (out_basis_far, out_basis),
        (neighbours_far, neighbours),
        (counts_far, counts),
        (admissible_far, admissible),
    ]
    small_copies = [
        pltpu.make_async_copy(source, target, small_sem.at[k])
        for k, (source, target) in enumerate(small)
    ]

    def tell(semaphore, to):
        pl.semaphore_signal(semaphore, inc=1, device_id={"leaf": to}, device_id_type=MESH)

    def direct(step):
        return step % 2 == 1

    far_steps = [step for step in range(3, chips) if direct(step)]
    small_copies[0].start()
    small_copies[1].start()
    own_copies[0].start()
    barrier = pltpu.get_barrier_semaphore()
    tell(barrier, sibling)

    @pl.when(last)
    def _():
        tell(barrier, (chip * 2 + 2) % n)
        tell(barrier, (chip * 2 + 3) % n)

    for step in range(2, chips):
        @pl.when((chip + step < chips) & (direct(step) | (core == 0) | (chip + step == chips - 1)))
        def _(step=step):
            tell(barrier, (me + 2 * step) % n)


    def cross_copy(k, part):
        leaf = core * (leaves - 1 - k) + (1 - core) * k
        return pltpu.make_async_remote_copy(
            src_ref=density.at[pl.ds(leaf, 1), pl.ds(part, 1)],
            dst_ref=halo.at[pl.ds(k, 1), pl.ds(part, 1)],
            send_sem=cross_send.at[2 * k + part],
            recv_sem=cross_recv.at[2 * k + part],
            device_id={"leaf": (me + n - 1 + 2 * core) % n},
            device_id_type=MESH,
        )

    def cross_start(which, begin, end):
        @pl.when((core == which) & ((first, last)[which]))
        def _():
            for piece in range(begin, end):
                cross_copy(piece // 2, piece % 2).start()

    crossing = ((core == 0) & first) | ((core == 1) & last)

    sib_copy = pltpu.make_async_remote_copy(
        src_ref=density.at[pl.ds((1 - core) * edge, HALO)],
        dst_ref=sib,
        send_sem=sib_send.at[0],
        recv_sem=sib_recv.at[0],
        device_id={"leaf": sibling},
        device_id_type=MESH,
    )

    for copy in own_copies[1:] + [small_copies[2]]:
        copy.start()
    def sends_down(step):
        return (chip >= step) & (direct(step) | (core == 0) | (chip == chips - 1))

    below = jnp.where(first, 2, 0)
    for step in range(2, chips):
        below += jnp.where(sends_down(step), 1, 0)
    pl.semaphore_wait(barrier, 1 + below)

    @pl.when(first)
    def _():
        tell(above_sem, (chip * 2 + n - 2) % n)
        tell(above_sem, (chip * 2 + n - 1) % n)

    for step in far_steps:
        @pl.when(chip >= step)
        def _(step=step):
            tell(far_sem, (me + n - 2 * step) % n)

    cross_start(0, 0, 3)
    small_copies[7].start()
    small_copies[8].start()
    for k in range(1, chunks - 1):
        tile_copies[k].start()
    small_copies[0].wait()
    small_copies[1].wait()

    def merge(leaf, carry):
        basis = leaf_basis[leaf]
        t_high, t_low = split(leaf_transfer[leaf].reshape(pair, rank))
        value = mul(
            jnp.concatenate([t_high, t_low], axis=0),
            jnp.concatenate([basis[0], basis[1]], axis=1),
        )
        value = value[:pair] + value[pair:]
        real = value[:rank, :panels] - value[rank:, panels:]
        imag = value[:rank, panels:] + value[rank:, :panels]
        high, low = split(embed(real, imag))
        merged[leaf, :pair] = high
        merged[leaf, pair:] = low
        return carry

    lax.fori_loop(0, leaves, merge, 0, unroll=True)

    root = jnp.zeros((2 * pair, rhs), F32)
    done = 0
    for count in (chunks // 2, chunks - chunks // 2):
        if done + count == chunks:
            @pl.when(last)
            def _():
                pl.semaphore_wait(above_sem, 2)

            cross_start(1, 0, 0)
        for k in range(done, done + count):
            own_copies[k].wait()
        begin, end = done * HALO, (done + count) * HALO
        left = jnp.concatenate([merged[leaf] for leaf in range(begin, end)], axis=1)
        root += mul(left, own[begin:end].reshape((end - begin) * size, rhs))
        done += count
    small_copies[2].wait()
    packed = jnp.concatenate([top_out[0, 0], top_out[0, 1]], axis=1).astype(BF16)
    msg[me, 2 * pair :] = jnp.concatenate([packed[: rank // 2], packed[rank // 2 :]], axis=1)
    root = (root[:pair] + root[pair:]).astype(BF16)
    msg[me, :pair] = root[:, : rhs // 2]
    msg[me, pair : 2 * pair] = root[:, rhs // 2 :]

    def root_copy(slot, send, recv, to):
        return pltpu.make_async_remote_copy(
            src_ref=msg.at[slot],
            dst_ref=msg.at[slot],
            send_sem=send,
            recv_sem=recv,
            device_id={"leaf": to},
            device_id_type=MESH,
        )

    def chip_of(step):
        return (chip + n + step) % chips

    def line_copy(way, step, hop):
        send = (up_send, down_send)[way]
        recv = (up_recv, down_recv)[way]
        sign = (1, -1)[way]
        slot = chip_of(-sign * step) * 2 + core
        to = chip_of(sign * hop) * 2 + core
        return root_copy(slot, send.at[step + hop], recv.at[step + hop], to)

    def below_of(way, step):
        return (chip >= step) if way == 0 else (chip + step < chips)

    def pass_copy(step):
        return root_copy(
            chip_of(step) * 2 + core,
            pass_send.at[step % chips],
            pass_recv.at[step % chips],
            sibling,
        )

    for step in reversed(range(1, chips)):
        @pl.when(sends_down(step))
        def _(step=step):
            line_copy(1, 0, step).start()

    @pl.when(last)
    def _():
        line_copy(0, 0, 1).start()

    pass_copy(0).start()

    cross_start(1, 0, 3)
    cross_start(0, 3, 6)
    sib_copy.start()

    small_copies[6].start()
    for copy in small_copies[3:6] + small_copies[9:]:
        copy.start()
    tile_copies[0].start()
    tile_copies[chunks - 1].start()

    def relays(way, step):
        if way == 1:
            return (chip + step < chips - 1) & first & (core == 1)
        return (chip >= step) & last

    def arrive(way, step):
        @pl.when(below_of(way, step))
        def _():
            line_copy(way, 0, step).wait_recv()
            pass_copy((-step, step)[way]).start()

        if direct(step) and step < chips - 1:
            @pl.when(relays(way, step))
            def _():
                line_copy(way, step, 1).start()

    begin = me * leaves

    def inside(slot, leaf):
        return own[jnp.clip(neighbours[slot, leaf] - begin, 0, leaves - 1)]

    def beside(slot, leaf):
        place = neighbours[slot, leaf] - (begin + (1 - core) * leaves - core * HALO)
        piece = sib[jnp.clip(place, 0, HALO - 1)]
        if not isinstance(slot, int):
            return piece
        return jnp.where((place >= 0) & (place < HALO), piece, inside(slot, leaf))

    def across(k):
        def piece(slot, leaf):
            value = inside(slot, leaf)
            for j in range(k + 1) if isinstance(slot, int) else [k]:
                place = begin + core * (leaves + j) - (1 - core) * (1 + j)
                value = jnp.where(neighbours[slot, leaf] == place, halo[j], value)
            return value

        return piece

    def product(leaf, chosen):
        tops, bottoms, pieces = [], [], []
        for slot, piece in chosen:
            real = tiles[leaf, slot, 0]
            imag = tiles[leaf, slot, 1]
            if isinstance(slot, int) and slot >= LIVE:
                live = jnp.where(counts[leaf] > slot, 1.0, 0.0).astype(F32)
                live = jnp.full((panels, panels), live, F32).astype(BF16)
                real *= live
                imag *= live
            tops += [real, -imag]
            bottoms += [imag, real]
            pieces.append(piece(slot, leaf).reshape(size, rhs))
        left = jnp.concatenate(
            [jnp.concatenate(tops, axis=1), jnp.concatenate(bottoms, axis=1)], axis=0
        )
        return mul(left, jnp.concatenate(pieces, axis=0))

    def near_leaf(chosen, start=0):
        def body(step, carry):
            near[start + step] = product(start + step, chosen)
            return carry

        return body

    open_slots = list(range(LIVE, slots))
    every = [(slot, inside) for slot in range(slots)]
    small_copies[7].wait()
    small_copies[8].wait()
    for k in range(1, chunks - 1):
        tile_copies[k].wait()
        lax.fori_loop(k * HALO, (k + 1) * HALO, near_leaf(every), 0, unroll=True)

    arrive(0, 1)
    above = jnp.int32(0)
    for step in far_steps:
        above += jnp.where(chip + step < chips, 1, 0)
    if far_steps:
        @pl.when(chip + 3 < chips)
        def _():
            pl.semaphore_wait(far_sem, above)

    for step in far_steps:
        @pl.when(chip + step < chips)
        def _(step=step):
            line_copy(0, 0, step).start()

    cross_start(1, 3, 2 * HALO)
    cross_start(0, 6, 7)

    tile_copies[0].wait()
    tile_copies[chunks - 1].wait()
    sib_copy.wait_recv()
    chosen = [(0, inside), (1 + core, inside), (2 - core, beside)]
    chosen += [(slot, beside) for slot in open_slots]
    lax.fori_loop(0, HALO, near_leaf(chosen, (1 - core) * edge), 0, unroll=True)

    small_copies[6].wait()

    def turn(leaf, carry):
        basis = out_basis[leaf].astype(F32)
        left = jnp.concatenate([basis[0], -basis[1]], axis=0)
        right = jnp.concatenate([basis[1], basis[0]], axis=0)
        turned[leaf] = jnp.concatenate([left, right], axis=1).T.astype(BF16)
        return carry

    lax.fori_loop(0, leaves, turn, 0, unroll=8)
    arrive(1, 1)
    cross_start(0, 7, 2 * HALO)

    for copy in small_copies[3:6] + small_copies[9:]:
        copy.wait()
    a_high, a_low = split(embed(top_in[0, 0], top_in[0, 1]))
    ones = lax.broadcasted_iota(jnp.int32, (pair, pair), 0) == lax.broadcasted_iota(
        jnp.int32, (pair, pair), 1
    )
    ones = jnp.where(ones, 1.0, 0.0).astype(BF16)
    spread = [
        jnp.concatenate([ones, a_high], axis=1),
        jnp.concatenate([jnp.zeros_like(ones), a_low], axis=1),
    ]
    some = HALO * pair

    def lower(k, carry):
        straight, turned_parts = [], []
        for i in range(HALO):
            real = down_transfer[k * HALO + i, 0].astype(BF16)
            imag = down_transfer[k * HALO + i, 1].astype(BF16)
            straight += [real, imag]
            turned_parts += [-imag, real]
        straight = jnp.concatenate(straight, axis=0)
        turned_parts = jnp.concatenate(turned_parts, axis=0)
        value = jnp.zeros((some, 2 * pair), F32)
        for right in spread:
            value += mul(straight, right[:rank]) + mul(turned_parts, right[rank:])
        rows = pl.ds(pl.multiple_of(k * some, some), some)
        downward[rows] = value.astype(BF16)
        return carry

    lax.fori_loop(0, chunks, lower, 0, unroll=True)

    for d in range(n):
        where = jnp.int32(0)
        found = jnp.int32(0)
        for slot in range(far):
            hit = admissible[0, slot] == d
            where = jnp.where(hit, slot, where)
            found = jnp.where(hit, 1, found)
        scale = found.astype(F32)
        weights[d] = pack(coupling[0, where, 0] * scale, coupling[0, where, 1] * scale)

    for step in range(2, chips):
        arrive(0, step)

    side = lax.broadcasted_iota(jnp.int32, (rank // 2, 4 * rank), 1) < pair
    side = jnp.where(side, 1.0, 0.0).astype(BF16)

    def terms(which):
        lefts, rights = [], []
        for slot in which:
            value = msg[slot]
            piece = value[2 * pair :]
            top = jnp.concatenate([piece * side, piece * (1 - side)], axis=0)
            value = jnp.concatenate([value[:pair], value[pair : 2 * pair]], axis=1)
            lefts.append(jnp.concatenate([weights[slot], top], axis=0))
            rights.append(operand(value[:rank], value[rank:pair]))
        return mul(jnp.concatenate(lefts, axis=1), jnp.concatenate(rights, axis=0))

    def other(step):
        return jnp.where(last, step, chips - step) % chips

    pass_copy(0).wait_recv()
    pass_copy(other(1)).wait_recv()
    beyond = (chip + other(1)) % chips
    partial[...] = terms([chip * 2, chip * 2 + 1, beyond * 2, beyond * 2 + 1])

    chosen = [(0, inside), (2 - core, inside)]
    lax.fori_loop(0, HALO, near_leaf(chosen, core * edge), 0, unroll=True)

    def cross_leaf(k):
        @pl.when(crossing)
        def _():
            cross_copy(k, 0).wait_recv()
            cross_copy(k, 1).wait_recv()

        leaf = core * (edge + k) + (1 - core) * (HALO - 1 - k)
        chosen = [(slot, across(k)) for slot in [1 + core] + open_slots]
        near[leaf] += product(leaf, chosen)

    early = (chip < chips // 2) | jnp.logical_not(crossing)

    @pl.when(early)
    def _():
        for k in range(HALO - 2):
            cross_leaf(k)

    for step in range(2, chips):
        arrive(1, step)

    @pl.when(early)
    def _():
        cross_leaf(HALO - 2)

    remote = [(chip + other(step)) % chips * 2 for step in range(2, chips)]
    if remote:
        partial[...] += terms([slot + core for slot in remote])
        for step in range(2, chips):
            pass_copy(other(step)).wait_recv()
    field = partial[...]
    if remote:
        field += terms([slot + 1 - core for slot in remote])
    stacked = jnp.concatenate(
        [field[:rank, :rhs], field[:rank, rhs:], field[rank:, :rhs], field[rank:, rhs:]], axis=0
    )
    x = downward[...]
    coefs[...] = mul(
        jnp.concatenate([x, x], axis=1), jnp.concatenate(split(stacked), axis=0)
    ).astype(BF16)

    @pl.when(jnp.logical_not(early))
    def _():
        for k in range(HALO - 1):
            cross_leaf(k)

    cross_leaf(HALO - 1)

    for k in range(HALO):
        @pl.when(crossing)
        def _(k=k):
            cross_copy(k, 0).wait_send()
            cross_copy(k, 1).wait_send()
    sib_copy.wait_send()
    for step in range(1, chips):
        @pl.when(sends_down(step))
        def _(step=step):
            line_copy(1, 0, step).wait_send()

    for step in range(1, chips, 2):
        @pl.when(chip + step < chips)
        def _(step=step):
            line_copy(0, 0, step).wait_send()

    for way in range(2):
        for step in range(1, chips - 1, 2):
            @pl.when(relays(way, step))
            def _(way=way, step=step):
                line_copy(way, step, 1).wait_send()
    for step in range(chips):
        pass_copy(step).wait_send()


def finish(near, coefs, turned, out, staged, sem):
    leaves, _, panels, rhs = out.shape
    pair = turned.shape[2]
    copies = []
    for k in range(leaves // 2):

        def body(leaf, carry):
            rows = pl.ds(pl.multiple_of(leaf * pair, pair), pair)
            value = mul(turned[leaf], coefs[rows]) + near[leaf]
            staged[leaf] = value.astype(BF16).reshape(2, panels, rhs)
            return carry

        lax.fori_loop(k * 2, (k + 1) * 2, body, 0, unroll=True)
        piece = pl.ds(k * 2, 2)
        copies.append(pltpu.make_async_copy(staged.at[piece], out.at[piece], sem.at[k]))
        copies[-1].start()
    for copy in copies:
        copy.wait()


def shards(*args):
    density, near_tiles = args[0], args[1]
    leaf_basis = args[4]
    n = lax.axis_size("leaf")
    leaves, _, panels, rhs = density.shape
    rank = leaf_basis.shape[2]
    pair = 2 * rank
    chips = n // 2
    chunks = leaves // HALO
    hbm = pl.BlockSpec(memory_space=pltpu.HBM)
    vmem = pl.BlockSpec(memory_space=pltpu.VMEM)
    dma = pltpu.SemaphoreType.DMA
    operands = [args[2].T if k == 2 else arg for k, arg in enumerate(args)]
    for k in range(len(operands)):
        operands[k] = pltpu.with_memory_space_constraint(operands[k], pltpu.HBM)
    middle = pl.pallas_call(
        functools.partial(kernel, n),
        out_shape=(
            jax.ShapeDtypeStruct((leaves, 2 * panels, rhs), F32),
            jax.ShapeDtypeStruct((leaves * pair, rhs), BF16),
            jax.ShapeDtypeStruct((leaves, 2 * panels, pair), BF16),
        ),
        in_specs=[hbm] * len(operands),
        out_specs=(vmem, vmem, vmem),
        scratch_shapes=[
            (pltpu.SMEM if k in INDICES else pltpu.VMEM)(operands[k].shape, operands[k].dtype)
            for k in range(2, len(operands))
        ]
        + [
            pltpu.VMEM((leaves, 2 * pair, 2 * panels), BF16),
            pltpu.VMEM((leaves * pair, 2 * pair), BF16),
            pltpu.VMEM((n, rank, 4 * rank), BF16),
            pltpu.VMEM((pair, 2 * rhs), F32),
            pltpu.VMEM(density.shape, BF16),
            pltpu.VMEM((HALO,) + density.shape[1:], BF16),
            pltpu.VMEM((HALO,) + density.shape[1:], BF16),
            pltpu.VMEM(near_tiles.shape, BF16),
            pltpu.VMEM((n, 2 * pair + rank // 2, rhs // 2), BF16),
            dma((len(operands) - 2,)),
            dma((chunks,)),
            dma((chunks,)),
            dma((2 * HALO,)),
            dma((2 * HALO,)),
            dma((1,)),
            dma((1,)),
            dma((chips,)),
            dma((chips,)),
            dma((chips,)),
            dma((chips,)),
            dma((chips,)),
            dma((chips,)),
            pltpu.SemaphoreType.REGULAR,
            pltpu.SemaphoreType.REGULAR,
        ],
        compiler_params=pltpu.CompilerParams(
            collective_id=0, has_side_effects=True, vmem_limit_bytes=36 * 1024 * 1024
        ),
        name="exchange",
    )(*operands)
    return pl.pallas_call(
        finish,
        out_shape=jax.ShapeDtypeStruct(density.shape, BF16),
        in_specs=[vmem] * 3,
        out_specs=hbm,
        scratch_shapes=[pltpu.VMEM(density.shape, BF16), dma((leaves // 2,))],
        compiler_params=pltpu.CompilerParams(vmem_limit_bytes=16 * 1024 * 1024),
        name="finish",
    )(*middle)


def solution(mesh):
    in_specs = (
        P("leaf", "node", None, None),
        P("leaf", None, "node", None, None),
        P("leaf", None),
        P("leaf"),
        P("leaf", "node", None, None),
        P("leaf", "node", None, None),
        P("leaf", None),
        P("leaf", "node", None, None),
        P("leaf", "node", None, None),
        P("leaf", None, "node", None, None),
        P("leaf", "node", None, None),
        P("leaf", "node", None, None),
    )
    out_specs = P("leaf", "node", None, None)
    return jax.shard_map(shards, mesh=mesh, in_specs=in_specs, out_specs=out_specs, check_vma=False)
```

```python
import functools

import jax
import jax.numpy as jnp
from jax import lax
from jax.experimental import pallas as pl
from jax.experimental.pallas import tpu as pltpu
from jax.sharding import PartitionSpec as P

HALO = 4
LIVE = 3
INDICES = (2, 3, 6)
MESH = pl.DeviceIdType.MESH
F32 = jnp.float32
BF16 = jnp.bfloat16


def mul(left, right):
    return jnp.dot(left, right, preferred_element_type=F32)


def split(x):
    high = x.astype(BF16)
    return high, (x - high.astype(F32)).astype(BF16)


def pack(real, imag):
    rh, rl = split(real)
    ih, il = split(imag)
    return jnp.concatenate([rh, ih, rl, il], axis=1)


def operand(real, imag):
    minus = -imag
    left = jnp.concatenate([real, minus, real, minus], axis=0)
    right = jnp.concatenate([imag, real, imag, real], axis=0)
    return jnp.concatenate([left, right], axis=1)


def embed(real, imag):
    return jnp.concatenate(
        [jnp.concatenate([real, -imag], axis=1), jnp.concatenate([imag, real], axis=1)], axis=0
    )


def kernel(
    n,
    density,
    near_tiles,
    neighbours_far,
    counts_far,
    leaf_basis_far,
    leaf_transfer_far,
    admissible_far,
    top_out_far,
    top_in_far,
    coupling_far,
    down_transfer_far,
    out_basis_far,
    near,
    coefs,
    turned,
    neighbours,
    counts,
    leaf_basis,
    leaf_transfer,
    admissible,
    top_out,
    top_in,
    coupling,
    down_transfer,
    out_basis,
    merged,
    downward,
    weights,
    partial,
    own,
    halo,
    sib,
    tiles,
    msg,
    small_sem,
    own_sem,
    tile_sem,
    cross_send,
    cross_recv,
    sib_send,
    sib_recv,
    up_send,
    up_recv,
    down_send,
    down_recv,
    pass_send,
    pass_recv,
    above_sem,
    far_sem,
):
    me = lax.axis_index("leaf")
    chips = n // 2
    chip = me // 2
    core = me % 2
    sibling = chip * 2 + (1 - core)
    leaves, _, panels, rhs = density.shape
    slots = near_tiles.shape[1]
    rank = leaf_basis.shape[2]
    far = coupling.shape[1]
    size = 2 * panels
    pair = 2 * rank
    chunks = leaves // HALO
    edge = leaves - HALO
    first = chip > 0
    last = chip < chips - 1

    own_copies = [
        pltpu.make_async_copy(
            density.at[pl.ds(k * HALO, HALO)], own.at[pl.ds(k * HALO, HALO)], own_sem.at[k]
        )
        for k in range(chunks)
    ]
    tile_copies = [
        pltpu.make_async_copy(
            near_tiles.at[pl.ds(k * HALO, HALO)], tiles.at[pl.ds(k * HALO, HALO)], tile_sem.at[k]
        )
        for k in range(chunks)
    ]

    small = [
        (leaf_basis_far, leaf_basis),
        (leaf_transfer_far, leaf_transfer),
        (top_out_far, top_out),
        (top_in_far, top_in),
        (coupling_far, coupling),
        (down_transfer_far, down_transfer),
        (out_basis_far, out_basis),
        (neighbours_far, neighbours),
        (counts_far, counts),
        (admissible_far, admissible),
    ]
    small_copies = [
        pltpu.make_async_copy(source, target, small_sem.at[k])
        for k, (source, target) in enumerate(small)
    ]

    def tell(semaphore, to):
        pl.semaphore_signal(semaphore, inc=1, device_id={"leaf": to}, device_id_type=MESH)

    def direct(step):
        return step % 2 == 1

    far_steps = [step for step in range(3, chips) if direct(step)]
    small_copies[0].start()
    small_copies[1].start()
    own_copies[0].start()
    barrier = pltpu.get_barrier_semaphore()
    tell(barrier, sibling)

    @pl.when(last)
    def _():
        tell(barrier, (chip * 2 + 2) % n)
        tell(barrier, (chip * 2 + 3) % n)

    for step in range(2, chips):
        @pl.when((chip + step < chips) & (direct(step) | (core == 0) | (chip + step == chips - 1)))
        def _(step=step):
            tell(barrier, (me + 2 * step) % n)


    def cross_copy(k, part, source=density):
        leaf = core * (leaves - 1 - k) + (1 - core) * k
        return pltpu.make_async_remote_copy(
            src_ref=source.at[pl.ds(leaf, 1), pl.ds(part, 1)],
            dst_ref=halo.at[pl.ds(k, 1), pl.ds(part, 1)],
            send_sem=cross_send.at[2 * k + part],
            recv_sem=cross_recv.at[2 * k + part],
            device_id={"leaf": (me + n - 1 + 2 * core) % n},
            device_id_type=MESH,
        )

    def cross_start(which, begin, end, source=own):
        @pl.when((core == which) & ((first, last)[which]))
        def _():
            for piece in range(begin, end):
                cross_copy(piece // 2, piece % 2, source).start()

    crossing = ((core == 0) & first) | ((core == 1) & last)

    sib_copy = pltpu.make_async_remote_copy(
        src_ref=own.at[pl.ds((1 - core) * edge, HALO)],
        dst_ref=sib,
        send_sem=sib_send.at[0],
        recv_sem=sib_recv.at[0],
        device_id={"leaf": sibling},
        device_id_type=MESH,
    )

    for copy in own_copies[1:] + [small_copies[2]]:
        copy.start()
    def sends_down(step):
        return (chip >= step) & (direct(step) | (core == 0) | (chip == chips - 1))

    below = jnp.where(first, 2, 0)
    for step in range(2, chips):
        below += jnp.where(sends_down(step), 1, 0)
    pl.semaphore_wait(barrier, 1 + below)

    @pl.when(first)
    def _():
        tell(above_sem, (chip * 2 + n - 2) % n)
        tell(above_sem, (chip * 2 + n - 1) % n)

    for step in far_steps:
        @pl.when(chip >= step)
        def _(step=step):
            tell(far_sem, (me + n - 2 * step) % n)

    cross_start(0, 0, 3, density)
    small_copies[7].start()
    small_copies[8].start()
    small_copies[0].wait()
    small_copies[1].wait()

    def merge(leaf, carry):
        basis = leaf_basis[leaf]
        t_high, t_low = split(leaf_transfer[leaf].reshape(pair, rank))
        value = mul(
            jnp.concatenate([t_high, t_low], axis=0),
            jnp.concatenate([basis[0], basis[1]], axis=1),
        )
        value = value[:pair] + value[pair:]
        real = value[:rank, :panels] - value[rank:, panels:]
        imag = value[:rank, panels:] + value[rank:, :panels]
        high, low = split(embed(real, imag))
        merged[leaf, :pair] = high
        merged[leaf, pair:] = low
        return carry

    lax.fori_loop(0, leaves, merge, 0, unroll=True)

    root = jnp.zeros((2 * pair, rhs), F32)
    done = 0
    for count in (chunks // 2, chunks - chunks // 2):
        if done + count == chunks:
            for k in range(1, chunks - 1):
                tile_copies[k].start()

            @pl.when(last)
            def _():
                pl.semaphore_wait(above_sem, 2)

            cross_start(1, 0, 1, density)

        for k in range(done, done + count):
            own_copies[k].wait()
        begin, end = done * HALO, (done + count) * HALO
        left = jnp.concatenate([merged[leaf] for leaf in range(begin, end)], axis=1)
        root += mul(left, own[begin:end].reshape((end - begin) * size, rhs))
        done += count
    small_copies[2].wait()
    packed = jnp.concatenate([top_out[0, 0], top_out[0, 1]], axis=1).astype(BF16)
    msg[me, 2 * pair :] = jnp.concatenate([packed[: rank // 2], packed[rank // 2 :]], axis=1)
    root = (root[:pair] + root[pair:]).astype(BF16)
    msg[me, :pair] = root[:, : rhs // 2]
    msg[me, pair : 2 * pair] = root[:, rhs // 2 :]

    def root_copy(slot, send, recv, to):
        return pltpu.make_async_remote_copy(
            src_ref=msg.at[slot],
            dst_ref=msg.at[slot],
            send_sem=send,
            recv_sem=recv,
            device_id={"leaf": to},
            device_id_type=MESH,
        )

    def chip_of(step):
        return (chip + n + step) % chips

    def line_copy(way, step, hop):
        send = (up_send, down_send)[way]
        recv = (up_recv, down_recv)[way]
        sign = (1, -1)[way]
        slot = chip_of(-sign * step) * 2 + core
        to = chip_of(sign * hop) * 2 + core
        return root_copy(slot, send.at[step + hop], recv.at[step + hop], to)

    def below_of(way, step):
        return (chip >= step) if way == 0 else (chip + step < chips)

    def pass_copy(step):
        return root_copy(
            chip_of(step) * 2 + core,
            pass_send.at[step % chips],
            pass_recv.at[step % chips],
            sibling,
        )

    for step in reversed(range(1, chips)):
        @pl.when(sends_down(step))
        def _(step=step):
            line_copy(1, 0, step).start()

    @pl.when(last)
    def _():
        line_copy(0, 0, 1).start()

    pass_copy(0).start()

    cross_start(1, 1, 4)
    cross_start(0, 3, 6)
    sib_copy.start()

    small_copies[6].start()
    for copy in small_copies[3:6] + small_copies[9:]:
        copy.start()
    tile_copies[0].start()
    tile_copies[chunks - 1].start()

    def relays(way, step):
        if way == 1:
            return (chip + step < chips - 1) & first & (core == 1)
        return (chip >= step) & last

    def arrive(way, step):
        @pl.when(below_of(way, step))
        def _():
            line_copy(way, 0, step).wait_recv()
            pass_copy((-step, step)[way]).start()

        if direct(step) and step < chips - 1:
            @pl.when(relays(way, step))
            def _():
                line_copy(way, step, 1).start()

    begin = me * leaves

    def inside(slot, leaf):
        return own[jnp.clip(neighbours[slot, leaf] - begin, 0, leaves - 1)]

    def beside(slot, leaf):
        place = neighbours[slot, leaf] - (begin + (1 - core) * leaves - core * HALO)
        piece = sib[jnp.clip(place, 0, HALO - 1)]
        if not isinstance(slot, int):
            return piece
        return jnp.where((place >= 0) & (place < HALO), piece, inside(slot, leaf))

    def across(k):
        def piece(slot, leaf):
            value = inside(slot, leaf)
            for j in range(k + 1) if isinstance(slot, int) else [k]:
                place = begin + core * (leaves + j) - (1 - core) * (1 + j)
                value = jnp.where(neighbours[slot, leaf] == place, halo[j], value)
            return value

        return piece

    def product(leaf, chosen):
        tops, bottoms, pieces = [], [], []
        for slot, piece in chosen:
            real = tiles[leaf, slot, 0]
            imag = tiles[leaf, slot, 1]
            if isinstance(slot, int) and slot >= LIVE:
                live = jnp.where(counts[leaf] > slot, 1.0, 0.0).astype(F32)
                live = jnp.full((panels, panels), live, F32).astype(BF16)
                real *= live
                imag *= live
            tops += [real, -imag]
            bottoms += [imag, real]
            pieces.append(piece(slot, leaf).reshape(size, rhs))
        left = jnp.concatenate(
            [jnp.concatenate(tops, axis=1), jnp.concatenate(bottoms, axis=1)], axis=0
        )
        return mul(left, jnp.concatenate(pieces, axis=0))

    def near_leaf(chosen, start=0):
        def body(step, carry):
            near[start + step] = product(start + step, chosen)
            return carry

        return body

    open_slots = list(range(LIVE, slots))
    every = [(slot, inside) for slot in range(slots)]
    small_copies[7].wait()
    small_copies[8].wait()
    for k in range(1, chunks - 1):
        tile_copies[k].wait()
        lax.fori_loop(k * HALO, (k + 1) * HALO, near_leaf(every), 0, unroll=True)

    arrive(0, 1)
    above = jnp.int32(0)
    for step in far_steps:
        above += jnp.where(chip + step < chips, 1, 0)
    if far_steps:
        @pl.when(chip + 3 < chips)
        def _():
            pl.semaphore_wait(far_sem, above)

    for step in far_steps:
        @pl.when(chip + step < chips)
        def _(step=step):
            line_copy(0, 0, step).start()

    cross_start(1, 4, 2 * HALO)
    cross_start(0, 6, 7)

    tile_copies[0].wait()
    tile_copies[chunks - 1].wait()
    sib_copy.wait_recv()
    chosen = [(0, inside), (1 + core, inside), (2 - core, beside)]
    chosen += [(slot, beside) for slot in open_slots]
    lax.fori_loop(0, HALO, near_leaf(chosen, (1 - core) * edge), 0, unroll=True)

    small_copies[6].wait()

    def turn(leaf, carry):
        basis = out_basis[leaf].astype(F32)
        left = jnp.concatenate([basis[0], -basis[1]], axis=0)
        right = jnp.concatenate([basis[1], basis[0]], axis=0)
        turned[leaf] = jnp.concatenate([left, right], axis=1).T.astype(BF16)
        return carry

    lax.fori_loop(0, leaves, turn, 0, unroll=8)
    arrive(1, 1)
    cross_start(0, 7, 2 * HALO)

    for copy in small_copies[3:6] + small_copies[9:]:
        copy.wait()
    a_high, a_low = split(embed(top_in[0, 0], top_in[0, 1]))
    ones = lax.broadcasted_iota(jnp.int32, (pair, pair), 0) == lax.broadcasted_iota(
        jnp.int32, (pair, pair), 1
    )
    ones = jnp.where(ones, 1.0, 0.0).astype(BF16)
    spread = [
        jnp.concatenate([ones, a_high], axis=1),
        jnp.concatenate([jnp.zeros_like(ones), a_low], axis=1),
    ]
    some = HALO * pair

    def lower(k, carry):
        straight, turned_parts = [], []
        for i in range(HALO):
            real = down_transfer[k * HALO + i, 0].astype(BF16)
            imag = down_transfer[k * HALO + i, 1].astype(BF16)
            straight += [real, imag]
            turned_parts += [-imag, real]
        straight = jnp.concatenate(straight, axis=0)
        turned_parts = jnp.concatenate(turned_parts, axis=0)
        value = jnp.zeros((some, 2 * pair), F32)
        for right in spread:
            value += mul(straight, right[:rank]) + mul(turned_parts, right[rank:])
        rows = pl.ds(pl.multiple_of(k * some, some), some)
        downward[rows] = value.astype(BF16)
        return carry

    lax.fori_loop(0, chunks, lower, 0, unroll=True)

    for d in range(n):
        where = jnp.int32(0)
        found = jnp.int32(0)
        for slot in range(far):
            hit = admissible[0, slot] == d
            where = jnp.where(hit, slot, where)
            found = jnp.where(hit, 1, found)
        scale = found.astype(F32)
        weights[d] = pack(coupling[0, where, 0] * scale, coupling[0, where, 1] * scale)

    chosen = [(0, inside), (2 - core, inside)]
    lax.fori_loop(0, HALO, near_leaf(chosen, core * edge), 0, unroll=True)

    for step in range(2, chips):
        arrive(0, step)

    side = lax.broadcasted_iota(jnp.int32, (rank // 2, 4 * rank), 1) < pair
    side = jnp.where(side, 1.0, 0.0).astype(BF16)

    def terms(which):
        lefts, rights = [], []
        for slot in which:
            value = msg[slot]
            piece = value[2 * pair :]
            top = jnp.concatenate([piece * side, piece * (1 - side)], axis=0)
            value = jnp.concatenate([value[:pair], value[pair : 2 * pair]], axis=1)
            lefts.append(jnp.concatenate([weights[slot], top], axis=0))
            rights.append(operand(value[:rank], value[rank:pair]))
        return mul(jnp.concatenate(lefts, axis=1), jnp.concatenate(rights, axis=0))

    def other(step):
        return jnp.where(last, step, chips - step) % chips

    pass_copy(0).wait_recv()
    pass_copy(other(1)).wait_recv()
    beyond = (chip + other(1)) % chips
    partial[...] = terms([chip * 2, chip * 2 + 1, beyond * 2, beyond * 2 + 1])


    def cross_leaf(k):
        @pl.when(crossing)
        def _():
            cross_copy(k, 0).wait_recv()
            cross_copy(k, 1).wait_recv()

        leaf = core * (edge + k) + (1 - core) * (HALO - 1 - k)
        chosen = [(slot, across(k)) for slot in [1 + core] + open_slots]
        near[leaf] += product(leaf, chosen)

    early = (chip < chips // 2) | jnp.logical_not(crossing)

    for k in range(HALO - 2):
        cross_leaf(k)

    for step in range(2, chips):
        arrive(1, step)

    ahead = jnp.logical_not(crossing)

    @pl.when(early)
    def _():
        cross_leaf(HALO - 2)

    @pl.when(ahead)
    def _():
        cross_leaf(HALO - 1)

    remote = [(chip + other(step)) % chips * 2 for step in range(2, chips)]
    if remote:
        partial[...] += terms([slot + core for slot in remote])
        for step in range(2, chips):
            pass_copy(other(step)).wait_recv()
    field = partial[...]
    if remote:
        field += terms([slot + 1 - core for slot in remote])
    stacked = jnp.concatenate(
        [field[:rank, :rhs], field[:rank, rhs:], field[rank:, :rhs], field[rank:, rhs:]], axis=0
    )
    x = downward[...]
    coefs[...] = mul(
        jnp.concatenate([x, x], axis=1), jnp.concatenate(split(stacked), axis=0)
    ).astype(BF16)

    @pl.when(jnp.logical_not(early))
    def _():
        cross_leaf(HALO - 2)

    @pl.when(jnp.logical_not(ahead))
    def _():
        cross_leaf(HALO - 1)

    for k in range(HALO):
        @pl.when(crossing)
        def _(k=k):
            cross_copy(k, 0).wait_send()
            cross_copy(k, 1).wait_send()
    sib_copy.wait_send()
    for step in range(1, chips):
        @pl.when(sends_down(step))
        def _(step=step):
            line_copy(1, 0, step).wait_send()

    for step in range(1, chips, 2):
        @pl.when(chip + step < chips)
        def _(step=step):
            line_copy(0, 0, step).wait_send()

    for way in range(2):
        for step in range(1, chips - 1, 2):
            @pl.when(relays(way, step))
            def _(way=way, step=step):
                line_copy(way, step, 1).wait_send()
    for step in range(chips):
        pass_copy(step).wait_send()


def finish(near, coefs, turned, out, staged, sem):
    leaves, _, panels, rhs = out.shape
    pair = turned.shape[2]
    copies = []
    for k in range(leaves // 2):

        def body(leaf, carry):
            rows = pl.ds(pl.multiple_of(leaf * pair, pair), pair)
            value = mul(turned[leaf], coefs[rows]) + near[leaf]
            staged[leaf] = value.astype(BF16).reshape(2, panels, rhs)
            return carry

        lax.fori_loop(k * 2, (k + 1) * 2, body, 0, unroll=True)
        piece = pl.ds(k * 2, 2)
        copies.append(pltpu.make_async_copy(staged.at[piece], out.at[piece], sem.at[k]))
        copies[-1].start()
    for copy in copies:
        copy.wait()


def shards(*args):
    density, near_tiles = args[0], args[1]
    leaf_basis = args[4]
    n = lax.axis_size("leaf")
    leaves, _, panels, rhs = density.shape
    rank = leaf_basis.shape[2]
    pair = 2 * rank
    chips = n // 2
    chunks = leaves // HALO
    hbm = pl.BlockSpec(memory_space=pltpu.HBM)
    vmem = pl.BlockSpec(memory_space=pltpu.VMEM)
    dma = pltpu.SemaphoreType.DMA
    operands = [args[2].T if k == 2 else arg for k, arg in enumerate(args)]
    for k in range(len(operands)):
        operands[k] = pltpu.with_memory_space_constraint(operands[k], pltpu.HBM)
    middle = pl.pallas_call(
        functools.partial(kernel, n),
        out_shape=(
            jax.ShapeDtypeStruct((leaves, 2 * panels, rhs), F32),
            jax.ShapeDtypeStruct((leaves * pair, rhs), BF16),
            jax.ShapeDtypeStruct((leaves, 2 * panels, pair), BF16),
        ),
        in_specs=[hbm] * len(operands),
        out_specs=(vmem, vmem, vmem),
        scratch_shapes=[
            (pltpu.SMEM if k in INDICES else pltpu.VMEM)(operands[k].shape, operands[k].dtype)
            for k in range(2, len(operands))
        ]
        + [
            pltpu.VMEM((leaves, 2 * pair, 2 * panels), BF16),
            pltpu.VMEM((leaves * pair, 2 * pair), BF16),
            pltpu.VMEM((n, rank, 4 * rank), BF16),
            pltpu.VMEM((pair, 2 * rhs), F32),
            pltpu.VMEM(density.shape, BF16),
            pltpu.VMEM((HALO,) + density.shape[1:], BF16),
            pltpu.VMEM((HALO,) + density.shape[1:], BF16),
            pltpu.VMEM(near_tiles.shape, BF16),
            pltpu.VMEM((n, 2 * pair + rank // 2, rhs // 2), BF16),
            dma((len(operands) - 2,)),
            dma((chunks,)),
            dma((chunks,)),
            dma((2 * HALO,)),
            dma((2 * HALO,)),
            dma((1,)),
            dma((1,)),
            dma((chips,)),
            dma((chips,)),
            dma((chips,)),
            dma((chips,)),
            dma((chips,)),
            dma((chips,)),
            pltpu.SemaphoreType.REGULAR,
            pltpu.SemaphoreType.REGULAR,
        ],
        compiler_params=pltpu.CompilerParams(
            collective_id=0, has_side_effects=True, vmem_limit_bytes=36 * 1024 * 1024
        ),
        name="exchange",
    )(*operands)
    return pl.pallas_call(
        finish,
        out_shape=jax.ShapeDtypeStruct(density.shape, BF16),
        in_specs=[vmem] * 3,
        out_specs=hbm,
        scratch_shapes=[pltpu.VMEM(density.shape, BF16), dma((leaves // 2,))],
        compiler_params=pltpu.CompilerParams(vmem_limit_bytes=16 * 1024 * 1024),
        name="finish",
    )(*middle)


def solution(mesh):
    in_specs = (
        P("leaf", "node", None, None),
        P("leaf", None, "node", None, None),
        P("leaf", None),
        P("leaf"),
        P("leaf", "node", None, None),
        P("leaf", "node", None, None),
        P("leaf", None),
        P("leaf", "node", None, None),
        P("leaf", "node", None, None),
        P("leaf", None, "node", None, None),
        P("leaf", "node", None, None),
        P("leaf", "node", None, None),
    )
    out_specs = P("leaf", "node", None, None)
    return jax.shard_map(shards, mesh=mesh, in_specs=in_specs, out_specs=out_specs, check_vma=False)
```

```python
import functools

import jax
import jax.numpy as jnp
from jax import lax
from jax.experimental import pallas as pl
from jax.experimental.pallas import tpu as pltpu
from jax.sharding import PartitionSpec as P

HALO = 4
LIVE = 3
INDICES = (2, 3, 6)
MESH = pl.DeviceIdType.MESH
F32 = jnp.float32
BF16 = jnp.bfloat16


def mul(left, right):
    return jnp.dot(left, right, preferred_element_type=F32)


def split(x):
    high = x.astype(BF16)
    return high, (x - high.astype(F32)).astype(BF16)


def pack(real, imag):
    rh, rl = split(real)
    ih, il = split(imag)
    return jnp.concatenate([rh, ih, rl, il], axis=1)


def operand(real, imag):
    minus = -imag
    left = jnp.concatenate([real, minus, real, minus], axis=0)
    right = jnp.concatenate([imag, real, imag, real], axis=0)
    return jnp.concatenate([left, right], axis=1)


def embed(real, imag):
    return jnp.concatenate(
        [jnp.concatenate([real, -imag], axis=1), jnp.concatenate([imag, real], axis=1)], axis=0
    )


def kernel(
    n,
    density,
    near_tiles,
    neighbours_far,
    counts_far,
    leaf_basis_far,
    leaf_transfer_far,
    admissible_far,
    top_out_far,
    top_in_far,
    coupling_far,
    down_transfer_far,
    out_basis_far,
    near,
    coefs,
    turned,
    neighbours,
    counts,
    leaf_basis,
    leaf_transfer,
    admissible,
    top_out,
    top_in,
    coupling,
    down_transfer,
    out_basis,
    merged,
    downward,
    weights,
    partial,
    own,
    halo,
    sib,
    tiles,
    msg,
    small_sem,
    own_sem,
    tile_sem,
    cross_send,
    cross_recv,
    sib_send,
    sib_recv,
    up_send,
    up_recv,
    down_send,
    down_recv,
    pass_send,
    pass_recv,
    above_sem,
    far_sem,
):
    me = lax.axis_index("leaf")
    chips = n // 2
    chip = me // 2
    core = me % 2
    sibling = chip * 2 + (1 - core)
    leaves, _, panels, rhs = density.shape
    slots = near_tiles.shape[1]
    rank = leaf_basis.shape[2]
    far = coupling.shape[1]
    size = 2 * panels
    pair = 2 * rank
    chunks = leaves // HALO
    edge = leaves - HALO
    first = chip > 0
    last = chip < chips - 1

    own_copies = [
        pltpu.make_async_copy(
            density.at[pl.ds(k * HALO, HALO)], own.at[pl.ds(k * HALO, HALO)], own_sem.at[k]
        )
        for k in range(chunks)
    ]
    tile_copies = [
        pltpu.make_async_copy(
            near_tiles.at[pl.ds(k * HALO, HALO)], tiles.at[pl.ds(k * HALO, HALO)], tile_sem.at[k]
        )
        for k in range(chunks)
    ]

    small = [
        (leaf_basis_far, leaf_basis),
        (leaf_transfer_far, leaf_transfer),
        (top_out_far, top_out),
        (top_in_far, top_in),
        (coupling_far, coupling),
        (down_transfer_far, down_transfer),
        (out_basis_far, out_basis),
        (neighbours_far, neighbours),
        (counts_far, counts),
        (admissible_far, admissible),
    ]
    small_copies = [
        pltpu.make_async_copy(source, target, small_sem.at[k])
        for k, (source, target) in enumerate(small)
    ]

    def tell(semaphore, to):
        pl.semaphore_signal(semaphore, inc=1, device_id={"leaf": to}, device_id_type=MESH)

    def direct(step):
        return step % 2 == 1

    far_steps = [step for step in range(3, chips) if direct(step)]
    small_copies[0].start()
    small_copies[1].start()
    own_copies[0].start()
    barrier = pltpu.get_barrier_semaphore()
    tell(barrier, sibling)

    @pl.when(last)
    def _():
        tell(barrier, (chip * 2 + 2) % n)
        tell(barrier, (chip * 2 + 3) % n)

    for step in range(2, chips):
        @pl.when((chip + step < chips) & (direct(step) | (core == 0) | (chip + step == chips - 1)))
        def _(step=step):
            tell(barrier, (me + 2 * step) % n)


    def cross_copy(k, part, source=density):
        leaf = core * (leaves - 1 - k) + (1 - core) * k
        return pltpu.make_async_remote_copy(
            src_ref=source.at[pl.ds(leaf, 1), pl.ds(part, 1)],
            dst_ref=halo.at[pl.ds(k, 1), pl.ds(part, 1)],
            send_sem=cross_send.at[2 * k + part],
            recv_sem=cross_recv.at[2 * k + part],
            device_id={"leaf": (me + n - 1 + 2 * core) % n},
            device_id_type=MESH,
        )

    def cross_start(which, begin, end, source=own):
        @pl.when((core == which) & ((first, last)[which]))
        def _():
            for piece in range(begin, end):
                cross_copy(piece // 2, piece % 2, source).start()

    crossing = ((core == 0) & first) | ((core == 1) & last)

    sib_copy = pltpu.make_async_remote_copy(
        src_ref=own.at[pl.ds((1 - core) * edge, HALO)],
        dst_ref=sib,
        send_sem=sib_send.at[0],
        recv_sem=sib_recv.at[0],
        device_id={"leaf": sibling},
        device_id_type=MESH,
    )

    for copy in own_copies[1:] + [small_copies[2]]:
        copy.start()
    def sends_down(step):
        return (chip >= step) & (direct(step) | (core == 0) | (chip == chips - 1))

    below = jnp.where(first, 2, 0)
    for step in range(2, chips):
        below += jnp.where(sends_down(step), 1, 0)
    pl.semaphore_wait(barrier, 1 + below)

    @pl.when(first)
    def _():
        tell(above_sem, (chip * 2 + n - 2) % n)
        tell(above_sem, (chip * 2 + n - 1) % n)

    for step in far_steps:
        @pl.when(chip >= step)
        def _(step=step):
            tell(far_sem, (me + n - 2 * step) % n)

    cross_start(0, 0, 3, density)
    small_copies[7].start()
    small_copies[8].start()
    small_copies[0].wait()
    small_copies[1].wait()

    def merge(leaf, carry):
        basis = leaf_basis[leaf]
        t_high, t_low = split(leaf_transfer[leaf].reshape(pair, rank))
        value = mul(
            jnp.concatenate([t_high, t_low], axis=0),
            jnp.concatenate([basis[0], basis[1]], axis=1),
        )
        value = value[:pair] + value[pair:]
        real = value[:rank, :panels] - value[rank:, panels:]
        imag = value[:rank, panels:] + value[rank:, :panels]
        high, low = split(embed(real, imag))
        merged[leaf, :pair] = high
        merged[leaf, pair:] = low
        return carry

    lax.fori_loop(0, leaves, merge, 0, unroll=True)

    root = jnp.zeros((2 * pair, rhs), F32)
    done = 0
    for count in (chunks // 2, chunks - chunks // 2):
        if done + count == chunks:
            for k in range(1, chunks - 1):
                tile_copies[k].start()

            @pl.when(last)
            def _():
                pl.semaphore_wait(above_sem, 2)

            cross_start(1, 0, 1, density)

        for k in range(done, done + count):
            own_copies[k].wait()
        begin, end = done * HALO, (done + count) * HALO
        left = jnp.concatenate([merged[leaf] for leaf in range(begin, end)], axis=1)
        root += mul(left, own[begin:end].reshape((end - begin) * size, rhs))
        done += count
    small_copies[2].wait()
    packed = jnp.concatenate([top_out[0, 0], top_out[0, 1]], axis=1).astype(BF16)
    msg[me, 2 * pair :] = jnp.concatenate([packed[: rank // 2], packed[rank // 2 :]], axis=1)
    root = (root[:pair] + root[pair:]).astype(BF16)
    msg[me, :pair] = root[:, : rhs // 2]
    msg[me, pair : 2 * pair] = root[:, rhs // 2 :]

    def root_copy(slot, send, recv, to):
        return pltpu.make_async_remote_copy(
            src_ref=msg.at[slot],
            dst_ref=msg.at[slot],
            send_sem=send,
            recv_sem=recv,
            device_id={"leaf": to},
            device_id_type=MESH,
        )

    def chip_of(step):
        return (chip + n + step) % chips

    def line_copy(way, step, hop):
        send = (up_send, down_send)[way]
        recv = (up_recv, down_recv)[way]
        sign = (1, -1)[way]
        slot = chip_of(-sign * step) * 2 + core
        to = chip_of(sign * hop) * 2 + core
        return root_copy(slot, send.at[step + hop], recv.at[step + hop], to)

    def below_of(way, step):
        return (chip >= step) if way == 0 else (chip + step < chips)

    def pass_copy(step):
        return root_copy(
            chip_of(step) * 2 + core,
            pass_send.at[step % chips],
            pass_recv.at[step % chips],
            sibling,
        )

    for step in reversed(range(1, chips)):
        @pl.when(sends_down(step))
        def _(step=step):
            line_copy(1, 0, step).start()

    @pl.when(last)
    def _():
        line_copy(0, 0, 1).start()

    pass_copy(0).start()

    cross_start(1, 1, 4)
    cross_start(0, 3, 6)
    sib_copy.start()

    small_copies[6].start()
    for copy in small_copies[3:6] + small_copies[9:]:
        copy.start()
    tile_copies[0].start()
    tile_copies[chunks - 1].start()

    def relays(way, step):
        if way == 1:
            return (chip + step < chips - 1) & first & (core == 1)
        return (chip >= step) & last

    def arrive(way, step):
        @pl.when(below_of(way, step))
        def _():
            line_copy(way, 0, step).wait_recv()
            pass_copy((-step, step)[way]).start()

        if direct(step) and step < chips - 1:
            @pl.when(relays(way, step))
            def _():
                line_copy(way, step, 1).start()

    begin = me * leaves

    def inside(slot, leaf):
        return own[jnp.clip(neighbours[slot, leaf] - begin, 0, leaves - 1)]

    def beside(slot, leaf):
        place = neighbours[slot, leaf] - (begin + (1 - core) * leaves - core * HALO)
        piece = sib[jnp.clip(place, 0, HALO - 1)]
        if not isinstance(slot, int):
            return piece
        return jnp.where((place >= 0) & (place < HALO), piece, inside(slot, leaf))

    def across(k):
        def piece(slot, leaf):
            value = inside(slot, leaf)
            for j in range(k + 1) if isinstance(slot, int) else [k]:
                place = begin + core * (leaves + j) - (1 - core) * (1 + j)
                value = jnp.where(neighbours[slot, leaf] == place, halo[j], value)
            return value

        return piece

    def product(leaf, chosen):
        tops, bottoms, pieces = [], [], []
        for slot, piece in chosen:
            real = tiles[leaf, slot, 0]
            imag = tiles[leaf, slot, 1]
            if isinstance(slot, int) and slot >= LIVE:
                live = jnp.where(counts[leaf] > slot, 1.0, 0.0).astype(F32)
                live = jnp.full((panels, panels), live, F32).astype(BF16)
                real *= live
                imag *= live
            tops += [real, -imag]
            bottoms += [imag, real]
            pieces.append(piece(slot, leaf).reshape(size, rhs))
        left = jnp.concatenate(
            [jnp.concatenate(tops, axis=1), jnp.concatenate(bottoms, axis=1)], axis=0
        )
        return mul(left, jnp.concatenate(pieces, axis=0))

    def near_leaf(chosen, start=0):
        def body(step, carry):
            near[start + step] = product(start + step, chosen)
            return carry

        return body

    open_slots = list(range(LIVE, slots))
    every = [(slot, inside) for slot in range(slots)]
    small_copies[7].wait()
    small_copies[8].wait()
    for k in range(1, chunks - 1):
        tile_copies[k].wait()
        lax.fori_loop(k * HALO, (k + 1) * HALO, near_leaf(every), 0, unroll=True)

    arrive(0, 1)
    above = jnp.int32(0)
    for step in far_steps:
        above += jnp.where(chip + step < chips, 1, 0)
    if far_steps:
        @pl.when(chip + 3 < chips)
        def _():
            pl.semaphore_wait(far_sem, above)

    for step in far_steps:
        @pl.when(chip + step < chips)
        def _(step=step):
            line_copy(0, 0, step).start()

    cross_start(1, 4, 2 * HALO)
    cross_start(0, 6, 7)

    tile_copies[0].wait()
    tile_copies[chunks - 1].wait()
    sib_copy.wait_recv()
    chosen = [(0, inside), (1 + core, inside), (2 - core, beside)]
    chosen += [(slot, beside) for slot in open_slots]
    lax.fori_loop(0, HALO, near_leaf(chosen, (1 - core) * edge), 0, unroll=True)

    small_copies[6].wait()

    def turn(leaf, carry):
        basis = out_basis[leaf].astype(F32)
        left = jnp.concatenate([basis[0], -basis[1]], axis=0)
        right = jnp.concatenate([basis[1], basis[0]], axis=0)
        turned[leaf] = jnp.concatenate([left, right], axis=1).T.astype(BF16)
        return carry

    lax.fori_loop(0, leaves, turn, 0, unroll=8)
    arrive(1, 1)
    cross_start(0, 7, 2 * HALO)

    for copy in small_copies[3:6] + small_copies[9:]:
        copy.wait()
    a_high, a_low = split(embed(top_in[0, 0], top_in[0, 1]))
    ones = lax.broadcasted_iota(jnp.int32, (pair, pair), 0) == lax.broadcasted_iota(
        jnp.int32, (pair, pair), 1
    )
    ones = jnp.where(ones, 1.0, 0.0).astype(BF16)
    spread = [
        jnp.concatenate([ones, a_high], axis=1),
        jnp.concatenate([jnp.zeros_like(ones), a_low], axis=1),
    ]
    some = HALO * pair

    def lower(k, carry):
        straight, turned_parts = [], []
        for i in range(HALO):
            real = down_transfer[k * HALO + i, 0].astype(BF16)
            imag = down_transfer[k * HALO + i, 1].astype(BF16)
            straight += [real, imag]
            turned_parts += [-imag, real]
        straight = jnp.concatenate(straight, axis=0)
        turned_parts = jnp.concatenate(turned_parts, axis=0)
        value = jnp.zeros((some, 2 * pair), F32)
        for right in spread:
            value += mul(straight, right[:rank]) + mul(turned_parts, right[rank:])
        rows = pl.ds(pl.multiple_of(k * some, some), some)
        downward[rows] = value.astype(BF16)
        return carry

    lax.fori_loop(0, chunks, lower, 0, unroll=True)

    for d in range(n):
        where = jnp.int32(0)
        found = jnp.int32(0)
        for slot in range(far):
            hit = admissible[0, slot] == d
            where = jnp.where(hit, slot, where)
            found = jnp.where(hit, 1, found)
        scale = found.astype(F32)
        weights[d] = pack(coupling[0, where, 0] * scale, coupling[0, where, 1] * scale)

    chosen = [(0, inside), (2 - core, inside)]
    lax.fori_loop(0, HALO, near_leaf(chosen, core * edge), 0, unroll=True)

    for step in range(2, chips):
        arrive(0, step)

    side = lax.broadcasted_iota(jnp.int32, (rank // 2, 4 * rank), 1) < pair
    side = jnp.where(side, 1.0, 0.0).astype(BF16)

    def terms(which):
        lefts, rights = [], []
        for slot in which:
            value = msg[slot]
            piece = value[2 * pair :]
            top = jnp.concatenate([piece * side, piece * (1 - side)], axis=0)
            value = jnp.concatenate([value[:pair], value[pair : 2 * pair]], axis=1)
            lefts.append(jnp.concatenate([weights[slot], top], axis=0))
            rights.append(operand(value[:rank], value[rank:pair]))
        return mul(jnp.concatenate(lefts, axis=1), jnp.concatenate(rights, axis=0))

    def other(step):
        return jnp.where(last, step, chips - step) % chips

    pass_copy(0).wait_recv()
    pass_copy(other(1)).wait_recv()
    beyond = (chip + other(1)) % chips
    partial[...] = terms([chip * 2, chip * 2 + 1, beyond * 2, beyond * 2 + 1])


    def cross_leaf(k):
        @pl.when(crossing)
        def _():
            cross_copy(k, 0).wait_recv()
            cross_copy(k, 1).wait_recv()

        leaf = core * (edge + k) + (1 - core) * (HALO - 1 - k)
        chosen = [(slot, across(k)) for slot in [1 + core] + open_slots]
        near[leaf] += product(leaf, chosen)

    early = (chip < chips // 2) | jnp.logical_not(crossing)

    for k in range(HALO - 2):
        cross_leaf(k)

    for step in range(2, chips):
        arrive(1, step)

    ahead = jnp.logical_not(crossing)

    @pl.when(early)
    def _():
        cross_leaf(HALO - 2)

    @pl.when(ahead)
    def _():
        cross_leaf(HALO - 1)

    remote = [(chip + other(step)) % chips * 2 for step in range(2, chips)]
    if remote:
        partial[...] += terms([slot + core for slot in remote])
        for step in range(2, chips):
            pass_copy(other(step)).wait_recv()
    field = partial[...]
    if remote:
        field += terms([slot + 1 - core for slot in remote])
    stacked = jnp.concatenate(
        [field[:rank, :rhs], field[:rank, rhs:], field[rank:, :rhs], field[rank:, rhs:]], axis=0
    )
    x = downward[...]
    coefs[...] = mul(
        jnp.concatenate([x, x], axis=1), jnp.concatenate(split(stacked), axis=0)
    ).astype(BF16)

    @pl.when(jnp.logical_not(early))
    def _():
        cross_leaf(HALO - 2)

    @pl.when(jnp.logical_not(ahead))
    def _():
        cross_leaf(HALO - 1)

    for k in range(HALO):
        @pl.when(crossing)
        def _(k=k):
            cross_copy(k, 0).wait_send()
            cross_copy(k, 1).wait_send()
    sib_copy.wait_send()
    for step in range(1, chips):
        @pl.when(sends_down(step))
        def _(step=step):
            line_copy(1, 0, step).wait_send()

    for step in range(1, chips, 2):
        @pl.when(chip + step < chips)
        def _(step=step):
            line_copy(0, 0, step).wait_send()

    for way in range(2):
        for step in range(1, chips - 1, 2):
            @pl.when(relays(way, step))
            def _(way=way, step=step):
                line_copy(way, step, 1).wait_send()
    for step in range(chips):
        pass_copy(step).wait_send()


def finish(near, coefs, turned, out, staged, sem):
    leaves, _, panels, rhs = out.shape
    pair = turned.shape[2]
    sizes = [1, 1, 2, 2, 2]
    sizes += [HALO] * ((leaves - sum(sizes)) // HALO)
    copies = []
    begin = 0
    for k, count in enumerate(sizes):
        for leaf in range(begin, begin + count):
            value = mul(turned[leaf], coefs[leaf * pair : (leaf + 1) * pair]) + near[leaf]
            staged[leaf] = value.astype(BF16).reshape(2, panels, rhs)
        piece = pl.ds(begin, count)
        copies.append(pltpu.make_async_copy(staged.at[piece], out.at[piece], sem.at[k]))
        copies[-1].start()
        begin += count
    for copy in copies:
        copy.wait()


def shards(*args):
    density, near_tiles = args[0], args[1]
    leaf_basis = args[4]
    n = lax.axis_size("leaf")
    leaves, _, panels, rhs = density.shape
    rank = leaf_basis.shape[2]
    pair = 2 * rank
    chips = n // 2
    chunks = leaves // HALO
    hbm = pl.BlockSpec(memory_space=pltpu.HBM)
    vmem = pl.BlockSpec(memory_space=pltpu.VMEM)
    dma = pltpu.SemaphoreType.DMA
    operands = [args[2].T if k == 2 else arg for k, arg in enumerate(args)]
    for k in range(len(operands)):
        operands[k] = pltpu.with_memory_space_constraint(operands[k], pltpu.HBM)
    middle = pl.pallas_call(
        functools.partial(kernel, n),
        out_shape=(
            jax.ShapeDtypeStruct((leaves, 2 * panels, rhs), F32),
            jax.ShapeDtypeStruct((leaves * pair, rhs), BF16),
            jax.ShapeDtypeStruct((leaves, 2 * panels, pair), BF16),
        ),
        in_specs=[hbm] * len(operands),
        out_specs=(vmem, vmem, vmem),
        scratch_shapes=[
            (pltpu.SMEM if k in INDICES else pltpu.VMEM)(operands[k].shape, operands[k].dtype)
            for k in range(2, len(operands))
        ]
        + [
            pltpu.VMEM((leaves, 2 * pair, 2 * panels), BF16),
            pltpu.VMEM((leaves * pair, 2 * pair), BF16),
            pltpu.VMEM((n, rank, 4 * rank), BF16),
            pltpu.VMEM((pair, 2 * rhs), F32),
            pltpu.VMEM(density.shape, BF16),
            pltpu.VMEM((HALO,) + density.shape[1:], BF16),
            pltpu.VMEM((HALO,) + density.shape[1:], BF16),
            pltpu.VMEM(near_tiles.shape, BF16),
            pltpu.VMEM((n, 2 * pair + rank // 2, rhs // 2), BF16),
            dma((len(operands) - 2,)),
            dma((chunks,)),
            dma((chunks,)),
            dma((2 * HALO,)),
            dma((2 * HALO,)),
            dma((1,)),
            dma((1,)),
            dma((chips,)),
            dma((chips,)),
            dma((chips,)),
            dma((chips,)),
            dma((chips,)),
            dma((chips,)),
            pltpu.SemaphoreType.REGULAR,
            pltpu.SemaphoreType.REGULAR,
        ],
        compiler_params=pltpu.CompilerParams(
            collective_id=0, has_side_effects=True, vmem_limit_bytes=36 * 1024 * 1024
        ),
        name="exchange",
    )(*operands)
    return pl.pallas_call(
        finish,
        out_shape=jax.ShapeDtypeStruct(density.shape, BF16),
        in_specs=[vmem] * 3,
        out_specs=hbm,
        scratch_shapes=[pltpu.VMEM(density.shape, BF16), dma((leaves // 2,))],
        compiler_params=pltpu.CompilerParams(vmem_limit_bytes=16 * 1024 * 1024),
        name="finish",
    )(*middle)


def solution(mesh):
    in_specs = (
        P("leaf", "node", None, None),
        P("leaf", None, "node", None, None),
        P("leaf", None),
        P("leaf"),
        P("leaf", "node", None, None),
        P("leaf", "node", None, None),
        P("leaf", None),
        P("leaf", "node", None, None),
        P("leaf", "node", None, None),
        P("leaf", None, "node", None, None),
        P("leaf", "node", None, None),
        P("leaf", "node", None, None),
    )
    out_specs = P("leaf", "node", None, None)
    return jax.shard_map(shards, mesh=mesh, in_specs=in_specs, out_specs=out_specs, check_vma=False)
```
